32 devices in a mesh: dp: 4 (over y, x), seq: 8 (over z, core).
Axes of the slice: x: 2, y: 2, z: 4, core: 2. Of those that a mesh axis runs over, the one named last changes fastest.
Arguments:
- tokens: bfloat16 [4, 2048, 2048], P('dp', 'seq'), may hold values from -6 to 6
- gain_attn: bfloat16 [2048], P(('dp', 'seq')), may hold values from 0.099609375 to 1.8984375
- w_query: bfloat16 [2048, 2048], P(('dp', 'seq')), may hold values from -0.1875 to 0.1875
- w_key: bfloat16 [2048, 512], P(('dp', 'seq')), may hold values from -0.125 to 0.125
- w_value: bfloat16 [2048, 512], P(('dp', 'seq')), may hold values from -0.125 to 0.125
- w_out: bfloat16 [2048, 2048], P(('dp', 'seq')), may hold values from -2 to 2
- gain_mlp: bfloat16 [2048], P(('dp', 'seq')), may hold values from 0.099609375 to 1.8984375
- w_gate: bfloat16 [2048, 8192], P('dp', 'seq'), may hold values from -0.125 to 0.125
- w_up: bfloat16 [2048, 8192], P('dp', 'seq'), may hold values from -0.125 to 0.125
- w_down: bfloat16 [2048, 8192], P('dp', 'seq'), may hold values from -0.0625 to 0.0625
- cotangent: bfloat16 [4, 2048, 2048], P('dp', 'seq'), may hold values from -6 to 6
Outputs:
- block_out: bfloat16 [4, 2048, 2048], P('dp', 'seq')
- grad_tokens: bfloat16 [4, 2048, 2048], P('dp', 'seq')
- grad_gain_attn: float32 [2048], P(('dp', 'seq'))
- grad_query: float32 [2048, 2048], P(('dp', 'seq'))
- grad_key: float32 [2048, 512], P(('dp', 'seq'))
- grad_value: float32 [2048, 512], P(('dp', 'seq'))
- grad_out: float32 [2048, 2048], P(('dp', 'seq'))
- grad_gain_mlp: float32 [2048], P(('dp', 'seq'))
- grad_gate: float32 [2048, 8192], P('dp', 'seq')
- grad_up: float32 [2048, 8192], P('dp', 'seq')
- grad_down: float32 [2048, 8192], P('dp', 'seq')
The draws below stay inside these ranges and needn't reach their ends.
All inputs are finite; a program needn't handle non-finite values.
Results may differ from the reference program's by a relative error of at most 0.017.
Values may be sent and summed in bfloat16 or wider, within the bound.
No kernel may reach another device: no remote copies, remote signals or barrier semaphores. Data moves between devices by JAX's collectives and lax.ppermute only.
A program may use at most 256 MiB of HBM per device.

```python
import jax
import jax.numpy as jnp
from jax import lax

D = 2048
FF = 8192
H = 32
KV = 8
HD = 64
LEN = 2048
BLOCK = 512
SEQS = 4


def with_spikes(array, own_key, source, target, parts, factor):
    def block_of(axis_at):
        return (jnp.arange(array.shape[axis_at]) // (array.shape[axis_at] // parts)).reshape((-1,) + (1,) * (array.ndim - 1 - axis_at))

    one_side = jax.random.permutation(own_key, parts)[block_of(target)]
    second = (block_of(target) + parts // 2) % parts
    return jnp.where((block_of(source) == one_side) | (block_of(source) == second), factor * array, array)


def block_scale(key, shape, shards, smallest, top_value):
    factor_of = 1.0
    for position, shards_of in shards:
        heights = jax.random.uniform(jax.random.fold_in(jax.random.fold_in(key, 6), position), (shards_of,), jnp.float32, smallest / len(shards), top_value / len(shards))
        factor_of = factor_of * jnp.repeat(jnp.exp(heights), shape[position] // shards_of).reshape((-1,) + (1,) * (len(shape) - 1 - position))
    return factor_of


def gaussian(own_key, dims, deviation, reach, cuts=(), held_as=jnp.bfloat16):
    loudness = block_scale(own_key, dims, cuts, -0.22, 0.18) if cuts else 1.0
    array = jax.random.normal(own_key, dims, jnp.float32) * deviation * loudness
    return jnp.minimum(jnp.maximum(array, -reach), reach).astype(held_as)


def noise_with(key, extent, width, most, shards, heavy, held_as=jnp.bfloat16):
    entries = width * jax.random.normal(key, extent, jnp.float32)
    if shards:
        entries = entries * block_scale(key, extent, shards, -0.22, 0.18)
    return jnp.clip(with_spikes(entries, jax.random.fold_in(key, 3), *heavy), -most, most).astype(held_as)


def setup_inputs(seed: int = 0) -> dict:
    splits = jax.random.split(jax.random.key(seed), 12)
    tokens = noise_with(splits[0], (SEQS, LEN, D), 1.0, 6.0, ((0, 4), (1, 8)), (1, 2, 8, 2.0))
    gain_attn = jnp.clip(1.0 + 0.18 * jax.random.normal(splits[1], (D,), jnp.float32), 0.099609375, 1.8984375).astype(jnp.bfloat16)
    w_query = gaussian(splits[2], (D, H * HD), (D // 2) ** -0.5, 0.1875, ((0, 32),))
    w_key = gaussian(splits[3], (D, KV * HD), D ** -0.5, 0.125, ((0, 32),))
    w_value = gaussian(splits[4], (D, KV * HD), D ** -0.5, 0.125, ((0, 32),))
    w_out = gaussian(splits[5], (H * HD, D), (max(D // 256, 1)) ** -0.5, 2.0, ((0, 32),))
    gain_mlp = jnp.clip(1.0 + 0.18 * jax.random.normal(splits[6], (D,), jnp.float32), 0.099609375, 1.8984375).astype(jnp.bfloat16)
    w_gate = gaussian(splits[7], (D, FF), D ** -0.5, 0.125, ((0, 4), (1, 8)))
    w_up = gaussian(splits[8], (D, FF), D ** -0.5, 0.125, ((0, 4), (1, 8)))
    w_down = gaussian(splits[9], (D, FF), FF ** -0.5, 0.0625, ((0, 4), (1, 8)))
    cotangent = noise_with(splits[10], (SEQS, LEN, D), 1.0, 6.0, ((0, 4), (1, 8)), (1, 2, 8, 2.0))
    return {"tokens": tokens, "gain_attn": gain_attn, "w_query": w_query, "w_key": w_key, "w_value": w_value, "w_out": w_out, "gain_mlp": gain_mlp, "w_gate": w_gate, "w_up": w_up, "w_down": w_down, "cotangent": cotangent}


@jax.custom_vjp
def low(v):
    return lax.optimization_barrier(v.astype(jnp.bfloat16)).astype(jnp.float32)

@jax.custom_vjp
def low_back(v):
    return v

def low_keep(v):
    return (low(v), None)

def low_pass(kept, grad):
    return (grad,)

def back_keep(v):
    return (v, None)

def back_low(kept, grad):
    return (low(grad),)
low.defvjp(low_keep, low_pass)
low_back.defvjp(back_keep, back_low)
epsilon = 1e-05
rope_theta = 500000.0
rope_factor = 32.0
old_context = 8192.0
highest = lax.Precision.HIGHEST

def frequencies(head_size):
    halves = jnp.arange(head_size // 2).astype(jnp.float32)
    plain = rope_theta ** (-2.0 * halves / head_size)
    blend = jnp.clip((old_context * plain / (2.0 * jnp.pi) - 1.0) / 3.0, 0.0, 1.0)
    return (1.0 - blend) * plain / rope_factor + blend * plain

def rope_tables(positions, head_size):
    angles = positions.astype(jnp.float32)[:, None] * frequencies(head_size)[None, :]
    return (jnp.cos(angles), jnp.sin(angles))

def rotate(heads_in, cosine_part, sine_part):
    half_size = heads_in.shape[-1] // 2
    first_half = heads_in[..., :half_size]
    second_half = heads_in[..., half_size:]
    cosine_wide = cosine_part[:, None, :]
    sine_wide = sine_part[:, None, :]
    return jnp.concatenate([first_half * cosine_wide - second_half * sine_wide, second_half * cosine_wide + first_half * sine_wide], axis=-1)

def norm_rows(values_in, gain_row):
    inverse = lax.rsqrt(lax.optimization_barrier(jnp.mean(values_in * values_in, axis=-1, keepdims=True)) + epsilon)
    return values_in * inverse * gain_row

def attention(queries, key_rows, value_rows):
    scale_factor = HD ** (-0.5)
    key_places = jnp.arange(LEN, dtype=jnp.int32)

    def one_block(block_index):
        first_row = (block_index * BLOCK).astype(jnp.int32)
        block_queries = lax.dynamic_slice_in_dim(queries, first_row, BLOCK, 0)
        scores = jnp.einsum('qhgd,khd->hgqk', block_queries, key_rows, precision=highest) * scale_factor
        scores = low_back(scores)
        query_places = first_row + jnp.arange(BLOCK, dtype=jnp.int32)
        allowed = key_places[None, :] <= query_places[:, None]
        scores = jnp.where(allowed, scores, -jnp.inf)
        row_peak = lax.optimization_barrier(jnp.max(scores, axis=-1, keepdims=True))
        exponent = jnp.exp(scores - row_peak)
        probabilities = exponent / lax.optimization_barrier(jnp.sum(exponent, axis=-1, keepdims=True))
        return jnp.einsum('hgqk,khd->qhgd', low(probabilities), value_rows, precision=highest)
    blocks = lax.map(jax.checkpoint(one_block), jnp.arange(LEN // BLOCK, dtype=jnp.int32))
    return blocks.reshape(LEN, H * HD)

def layer(sequence, gain_attn, w_query, w_key, w_value, w_out, gain_mlp, w_gate, w_up, w_down):
    cosine_part, sine_part = rope_tables(jnp.arange(LEN, dtype=jnp.int32), HD)
    normed = low(norm_rows(sequence, gain_attn))
    query_pre = low_back(jnp.dot(normed, w_query, precision=highest)).reshape(LEN, H, HD)
    key_pre = low_back(jnp.dot(normed, w_key, precision=highest)).reshape(LEN, KV, HD)
    value_rows = low(low_back(jnp.dot(normed, w_value, precision=highest))).reshape(LEN, KV, HD)
    queries = low(low_back(rotate(query_pre, cosine_part, sine_part))).reshape(LEN, KV, H // KV, HD)
    key_rows = low(low_back(rotate(key_pre, cosine_part, sine_part)))
    mixed = low(low_back(attention(queries, key_rows, value_rows)))
    middle = sequence + low_back(jnp.dot(mixed, w_out, precision=highest))
    normed_two = low(norm_rows(middle, gain_mlp))
    gate = low_back(jnp.dot(normed_two, w_gate, precision=highest))
    up_proj = low_back(jnp.dot(normed_two, w_up, precision=highest))
    hidden = low(gate * jax.nn.sigmoid(gate) * up_proj)
    return middle + jnp.dot(hidden, w_down.T, precision=highest)

def reference(tokens, gain_attn, w_query, w_key, w_value, w_out, gain_mlp, w_gate, w_up, w_down, cotangent):
    params = tuple((weight_array.astype(jnp.float32) for weight_array in (gain_attn, w_query, w_key, w_value, w_out, gain_mlp, w_gate, w_up, w_down)))

    def per_sequence(totals, pair):
        sequence, direction = pair
        output, pullback = jax.vjp(layer, sequence, *params)
        grads = pullback(direction)
        summed = tuple((running + fresh for running, fresh in zip(totals, grads[1:])))
        return (summed, (output, grads[0]))
    zeros = tuple((jnp.zeros(weight_array.shape, jnp.float32) for weight_array in params))
    totals, (outputs, input_grads) = lax.scan(per_sequence, zeros, (tokens.astype(jnp.float32), cotangent.astype(jnp.float32)))
    return (outputs.astype(jnp.bfloat16), input_grads.astype(jnp.bfloat16), totals[0], totals[1], totals[2], totals[3], totals[4], totals[5], totals[6], totals[7], totals[8])
```

```python
import functools

import jax
import jax.numpy as jnp
import numpy as np
from jax import lax
from jax.experimental import pallas as pl
from jax.experimental.pallas import tpu as pltpu
from jax.sharding import PartitionSpec as P

H = 32
KV = 8
HD = 64
LANES = 128
VMEM_BYTES = 50 * 2**20

epsilon = 1e-05
rope_theta = 500000.0
rope_factor = 32.0
old_context = 8192.0

f32 = jnp.float32
bf16 = jnp.bfloat16

NN = (((1,), (0,)), ((), ()))
NT = (((1,), (1,)), ((), ()))
TN = (((0,), (0,)), ((), ()))


def mm(a, b, dims):
    return lax.dot_general(a, b, dims, preferred_element_type=f32)


def cost(flops, moved, transcendentals=0):
    return pl.CostEstimate(flops=flops, bytes_accessed=moved, transcendentals=transcendentals)


def params():
    return pltpu.CompilerParams(vmem_limit_bytes=VMEM_BYTES)


def frequencies(head_size):
    halves = jnp.arange(head_size // 2).astype(f32)
    plain = rope_theta ** (-2.0 * halves / head_size)
    blend = jnp.clip((old_context * plain / (2.0 * jnp.pi) - 1.0) / 3.0, 0.0, 1.0)
    return (1.0 - blend) * plain / rope_factor + blend * plain


def rope_tables(length):
    freq = jnp.tile(frequencies(HD), LANES // (HD // 2))
    angles = jnp.arange(length).astype(f32)[:, None] * freq[None, :]
    sign = jnp.where((jnp.arange(LANES) % HD) < HD // 2, -1.0, 1.0).astype(f32)
    return jnp.cos(angles), jnp.sin(angles) * sign[None, :]


def turn(x, cos, sin):
    lane = lax.broadcasted_iota(jnp.int32, x.shape, 1)
    swapped = jnp.where(
        lane % HD < HD // 2, pltpu.roll(x, LANES - HD // 2, 1), pltpu.roll(x, HD // 2, 1)
    )
    return x * cos + swapped * sin


def qkv_kernel(width, mine, other, gain, w, cos, sin, normed, qkv):
    x = jnp.concatenate([mine[...], other[...]], axis=0).astype(f32)
    inverse = lax.rsqrt(jnp.mean(x * x, axis=-1, keepdims=True) + epsilon)
    low = (x * inverse * gain[...]).astype(bf16)
    normed[...] = low
    y = mm(low, w[...], NN)
    lane = lax.broadcasted_iota(jnp.int32, (x.shape[0], LANES), 1)
    for at in range(0, width + 2 * HD, LANES):
        part = y[:, at : at + LANES]
        turned = turn(part, cos[...], sin[...])
        if at >= width:
            turned = jnp.where(lane < HD, turned, part)
        qkv[:, at : at + LANES] = turned.astype(bf16)


def qkv_call(mine, other, gain, w, cos, sin, width):
    rows, depth = mine.shape
    cols = width + 2 * HD
    return pl.pallas_call(
        functools.partial(qkv_kernel, width),
        out_shape=[
            jax.ShapeDtypeStruct((2 * rows, depth), bf16),
            jax.ShapeDtypeStruct((2 * rows, cols), bf16),
        ],
        compiler_params=params(),
        cost_estimate=cost(4 * rows * depth * cols, 8 * rows * depth + 2 * depth * cols),
        name="qkv",
    )(mine, other, gain, w, cos, sin)


def fwd_kernel(bq, share, q_ref, kv_ref, out_ref, ot_ref, lse_ref, m_s, l_s, acc_s):
    i = pl.program_id(0)
    m_s[...] = jnp.full(m_s.shape, -1e30, f32)
    l_s[...] = jnp.zeros(l_s.shape, f32)
    acc_s[...] = jnp.zeros(acc_s.shape, f32)
    qs = q_ref[...] * jnp.asarray(HD**-0.5, bf16)

    def step(j, masked):
        start = pl.multiple_of(j * bq, bq)
        kk = kv_ref[pl.ds(start, bq), :HD]
        vv = kv_ref[pl.ds(start, bq), HD:]
        for h in range(share):
            at = slice(h * HD, (h + 1) * HD)
            s = mm(kk, qs[:, at], NT)
            if masked:
                ki = lax.broadcasted_iota(jnp.int32, s.shape, 0)
                qi = lax.broadcasted_iota(jnp.int32, s.shape, 1)
                s = jnp.where(ki <= qi, s, -1e30)
            m_old = m_s[h : h + 1, :]
            m_new = jnp.maximum(m_old, jnp.max(s, axis=0, keepdims=True))
            p = jnp.exp(s - m_new)
            alpha = jnp.exp(m_old - m_new)
            l_s[h : h + 1, :] = l_s[h : h + 1, :] * alpha + jnp.sum(p, axis=0, keepdims=True)
            m_s[h : h + 1, :] = m_new
            acc_s[at, :] = acc_s[at, :] * alpha + mm(vv, p.astype(bf16), TN)

    def plain(j, carry):
        step(j, False)
        return carry

    lax.fori_loop(0, i, plain, 0)
    step(i, True)
    for h in range(share):
        at = slice(h * HD, (h + 1) * HD)
        total = l_s[h : h + 1, :]
        ot_ref[at, :] = acc_s[at, :] / total
        lse_ref[h : h + 1, :] = m_s[h : h + 1, :] + jnp.log(total)
    out_ref[...] = ot_ref[...].T.astype(bf16)


def attn_fwd(q, kv, bq=1024):
    length, width = q.shape
    share = width // HD
    rows = max(8, share)
    return pl.pallas_call(
        functools.partial(fwd_kernel, bq, share),
        grid=(length // bq,),
        in_specs=[
            pl.BlockSpec((bq, width), lambda i: (i, 0)),
            pl.BlockSpec((length, 2 * HD), lambda i: (0, 0)),
        ],
        out_specs=[
            pl.BlockSpec((bq, width), lambda i: (i, 0)),
            pl.BlockSpec((width, bq), lambda i: (0, i)),
            pl.BlockSpec((rows, bq), lambda i: (0, i)),
        ],
        out_shape=[
            jax.ShapeDtypeStruct((length, width), bf16),
            jax.ShapeDtypeStruct((width, length), f32),
            jax.ShapeDtypeStruct((rows, length), f32),
        ],
        scratch_shapes=[
            pltpu.VMEM((rows, bq), f32),
            pltpu.VMEM((rows, bq), f32),
            pltpu.VMEM((width, bq), f32),
        ],
        compiler_params=params(),
        cost_estimate=cost(8 * length * length * width, 8 * length * width, share * length * length // 2),
        name="attn_fwd",
    )(q, kv)


def bwd_kernel(
    bq, share, q_ref, kv_ref, do_ref, ot_ref, lse_ref, cos_ref, sin_ref, dq_ref, dkv_ref, dqt_s, dk_s, dv_s
):
    i = pl.program_id(0)

    @pl.when(i == 0)
    def _():
        dk_s[...] = jnp.zeros(dk_s.shape, f32)
        dv_s[...] = jnp.zeros(dv_s.shape, f32)

    dqt_s[...] = jnp.zeros(dqt_s.shape, f32)
    qs = q_ref[...] * jnp.asarray(HD**-0.5, bf16)
    do = do_ref[...]
    product = do.astype(f32).T * ot_ref[...]
    inner = [jnp.sum(product[h * HD : (h + 1) * HD], axis=0, keepdims=True) for h in range(share)]

    def step(j, masked):
        start = pl.multiple_of(j * bq, bq)
        kk = kv_ref[pl.ds(start, bq), :HD]
        vv = kv_ref[pl.ds(start, bq), HD:]
        dk = jnp.zeros((bq, HD), f32)
        dv = jnp.zeros((bq, HD), f32)
        for h in range(share):
            at = slice(h * HD, (h + 1) * HD)
            s = mm(kk, qs[:, at], NT)
            p = jnp.exp(s - lse_ref[h : h + 1, :])
            if masked:
                ki = lax.broadcasted_iota(jnp.int32, s.shape, 0)
                qi = lax.broadcasted_iota(jnp.int32, s.shape, 1)
                p = jnp.where(ki <= qi, p, 0.0)
            dp = mm(vv, do[:, at], NT)
            ds = (p * (dp - inner[h])).astype(bf16)
            dv = dv + mm(p.astype(bf16), do[:, at], NN)
            dk = dk + mm(ds, qs[:, at], NN)
            dqt_s[at, :] += mm(kk, ds, TN)
        dk_s[pl.ds(start, bq), :] += dk
        dv_s[pl.ds(start, bq), :] += dv

    def plain(j, carry):
        step(j, False)
        return carry

    lax.fori_loop(0, i, plain, 0)
    step(i, True)
    dq = (dqt_s[...] * (HD**-0.5)).T.astype(bf16).astype(f32)
    rows = pl.ds(pl.multiple_of(i * bq, bq), bq)
    for at in range(0, share * HD, LANES):
        part = dq[:, at : at + LANES]
        dq_ref[:, at : at + LANES] = turn(part, cos_ref[rows, :], -sin_ref[rows, :]).astype(bf16)

    @pl.when(i == pl.num_programs(0) - 1)
    def _():
        both = jnp.concatenate([dk_s[...], dv_s[...]], axis=1).astype(bf16).astype(f32)
        lane = lax.broadcasted_iota(jnp.int32, both.shape, 1)
        turned = turn(both, cos_ref[...], -sin_ref[...])
        dkv_ref[...] = jnp.where(lane < HD, turned, both).astype(bf16)


def attn_bwd(q, kv, do, ot, lse, cos, sin, bq=512):
    length, width = q.shape
    share = width // HD
    rows = lse.shape[0]
    return pl.pallas_call(
        functools.partial(bwd_kernel, bq, share),
        grid=(length // bq,),
        in_specs=[
            pl.BlockSpec((bq, width), lambda i: (i, 0)),
            pl.BlockSpec((length, 2 * HD), lambda i: (0, 0)),
            pl.BlockSpec((bq, width), lambda i: (i, 0)),
            pl.BlockSpec((width, bq), lambda i: (0, i)),
            pl.BlockSpec((rows, bq), lambda i: (0, i)),
            pl.BlockSpec((length, LANES), lambda i: (0, 0)),
            pl.BlockSpec((length, LANES), lambda i: (0, 0)),
        ],
        out_specs=[
            pl.BlockSpec((bq, width), lambda i: (i, 0)),
            pl.BlockSpec((length, 2 * HD), lambda i: (0, 0)),
        ],
        out_shape=[
            jax.ShapeDtypeStruct((length, width), bf16),
            jax.ShapeDtypeStruct((length, 2 * HD), bf16),
        ],
        scratch_shapes=[
            pltpu.VMEM((width, bq), f32),
            pltpu.VMEM((length, HD), f32),
            pltpu.VMEM((length, HD), f32),
        ],
        compiler_params=params(),
        cost_estimate=cost(20 * length * length * width, 16 * length * width, share * length * length // 2),
        name="attn_bwd",
    )(q, kv, do, ot, lse, cos, sin)


def out_kernel(mixed, w, x, gain, middle, normed, acc):
    g = pl.program_id(0)

    @pl.when(g == 0)
    def _():
        acc[...] = x[...].astype(f32)

    acc[...] += mm(mixed[0], w[...], NN)

    @pl.when(g == pl.num_programs(0) - 1)
    def _():
        total = acc[...]
        middle[...] = total
        inverse = lax.rsqrt(jnp.mean(total * total, axis=-1, keepdims=True) + epsilon)
        normed[...] = (total * inverse * gain[...]).astype(bf16)


def out_call(mixed, w, x, gain):
    groups, rows, part = mixed.shape
    depth = w.shape[1]
    return pl.pallas_call(
        out_kernel,
        grid=(groups,),
        in_specs=[
            pl.BlockSpec((1, rows, part), lambda g: (g, 0, 0)),
            pl.BlockSpec((part, depth), lambda g: (g, 0)),
            pl.BlockSpec((rows, depth), lambda g: (0, 0)),
            pl.BlockSpec((1, depth), lambda g: (0, 0)),
        ],
        out_specs=[
            pl.BlockSpec((rows, depth), lambda g: (0, 0)),
            pl.BlockSpec((rows, depth), lambda g: (0, 0)),
        ],
        out_shape=[
            jax.ShapeDtypeStruct((rows, depth), f32),
            jax.ShapeDtypeStruct((rows, depth), bf16),
        ],
        scratch_shapes=[pltpu.VMEM((rows, depth), f32)],
        compiler_params=params(),
        cost_estimate=cost(2 * groups * part * rows * depth, 2 * groups * part * depth + 8 * rows * depth),
        name="out_norm",
    )(mixed, w, x, gain)


def ffn_kernel(
    x_mine, x_other, c_mine, c_other, w_gate, w_up, w_down,
    hidden, d_gate, d_up, back_mine, back_other, down_mine, down_other, back, down,
):
    u = pl.program_id(0)
    x = jnp.concatenate([x_mine[...], x_other[...]], axis=0)
    c = jnp.concatenate([c_mine[...], c_other[...]], axis=0)
    gate = mm(x, w_gate[...], NN)
    up = mm(x, w_up[...], NN)
    grad = mm(c, w_down[...], NN)
    sig = jax.nn.sigmoid(gate)
    silu = gate * sig
    act = (silu * up).astype(bf16)
    dg = (grad * up * sig * (1.0 + gate * (1.0 - sig))).astype(bf16)
    du = (grad * silu).astype(bf16)
    hidden[...] = act
    d_gate[...] = dg
    d_up[...] = du

    @pl.when(u == 0)
    def _():
        back[...] = mm(dg, w_gate[...], NT) + mm(du, w_up[...], NT)
        down[...] = mm(act, w_down[...], NT)

    @pl.when(u > 0)
    def _():
        back[...] += mm(dg, w_gate[...], NT) + mm(du, w_up[...], NT)
        down[...] += mm(act, w_down[...], NT)

    @pl.when(u == pl.num_programs(0) - 1)
    def _():
        rows = back_mine.shape[0]
        back_mine[...] = back[:rows].astype(bf16)
        back_other[...] = back[rows:].astype(bf16)
        down_mine[...] = down[:rows].astype(bf16)
        down_other[...] = down[rows:].astype(bf16)


def ffn_call(x_mine, x_other, c_mine, c_other, w_gate, w_up, w_down, tile=256):
    rows, depth = x_mine.shape
    units = w_gate.shape[1]
    block = pl.BlockSpec((rows, depth), lambda u: (0, 0))
    weight = pl.BlockSpec((depth, tile), lambda u: (0, u))
    act = pl.BlockSpec((2 * rows, tile), lambda u: (0, u))
    act_shape = jax.ShapeDtypeStruct((2 * rows, units), bf16)
    row_shape = jax.ShapeDtypeStruct((rows, depth), bf16)
    return pl.pallas_call(
        ffn_kernel,
        grid=(units // tile,),
        in_specs=[block] * 4 + [weight] * 3,
        out_specs=[act] * 3 + [block] * 4,
        out_shape=[act_shape] * 3 + [row_shape] * 4,
        scratch_shapes=[pltpu.VMEM((2 * rows, depth), f32)] * 2,
        compiler_params=params(),
        cost_estimate=cost(24 * rows * depth * units, 6 * depth * units + 20 * rows * depth + 12 * rows * units),
        name="ffn",
    )(x_mine, x_other, c_mine, c_other, w_gate, w_up, w_down)


def mid_kernel(got, own, middle, cot, gain, w, d_middle, branch, d_gain, d_mixed, low):
    @pl.when(pl.program_id(0) == 0)
    def _():
        grad = got[...].astype(f32) + own[...].astype(f32)
        m = middle[...]
        inverse = lax.rsqrt(jnp.mean(m * m, axis=-1, keepdims=True) + epsilon)
        scaled = grad * gain[...]
        slope = jnp.mean(m * scaled, axis=-1, keepdims=True) * (inverse * inverse * inverse)
        total = cot[...].astype(f32) + inverse * scaled - m * slope
        d_middle[...] = total
        branch[...] = total.astype(bf16)
        low[...] = total.astype(bf16)
        d_gain[...] = jnp.sum(grad * m * inverse, axis=0, keepdims=True)

    d_mixed[0] = mm(low[...], w[...], NT).astype(bf16)


def mid_call(got, own, middle, cot, gain, w, part):
    rows, depth = middle.shape
    groups = w.shape[0] // part
    block = pl.BlockSpec((rows, depth), lambda g: (0, 0))
    line = pl.BlockSpec((1, depth), lambda g: (0, 0))
    return pl.pallas_call(
        mid_kernel,
        grid=(groups,),
        in_specs=[block, block, block, block, line, pl.BlockSpec((part, depth), lambda g: (g, 0))],
        out_specs=[block, block, line, pl.BlockSpec((1, rows, part), lambda g: (g, 0, 0))],
        out_shape=[
            jax.ShapeDtypeStruct((rows, depth), f32),
            jax.ShapeDtypeStruct((rows, depth), bf16),
            jax.ShapeDtypeStruct((1, depth), f32),
            jax.ShapeDtypeStruct((groups, rows, part), bf16),
        ],
        scratch_shapes=[pltpu.VMEM((rows, depth), bf16)],
        compiler_params=params(),
        cost_estimate=cost(2 * groups * part * rows * depth, 2 * groups * part * depth + 16 * rows * depth),
        name="mid",
    )(got, own, middle, cot, gain, w)


def first_kernel(got, own, x_ref, d_middle, gain, out):
    grad = got[...].astype(f32) + own[...].astype(f32)
    x = x_ref[...].astype(f32)
    inverse = lax.rsqrt(jnp.mean(x * x, axis=-1, keepdims=True) + epsilon)
    scaled = grad * gain[...]
    slope = jnp.mean(x * scaled, axis=-1, keepdims=True) * (inverse * inverse * inverse)
    out[...] = (d_middle[...] + inverse * scaled - x * slope).astype(bf16)


def first_call(got, own, x, d_middle, gain):
    rows, depth = x.shape
    return pl.pallas_call(
        first_kernel,
        out_shape=jax.ShapeDtypeStruct((rows, depth), bf16),
        compiler_params=params(),
        cost_estimate=cost(20 * rows * depth, 12 * rows * depth),
        name="first_norm_back",
    )(got, own, x, d_middle, gain)


def after(value, *others):
    return lax.optimization_barrier((value,) + others)[0]


def shards(
    tokens, gain_attn, w_query, w_key, w_value, w_out, gain_mlp, w_gate, w_up, w_down, cotangent
):
    groups = lax.axis_size("seq")
    dp_count = lax.axis_size("dp")
    seq_count, piece, depth = tokens.shape
    assert seq_count == 1 and groups >= KV and groups % 2 == 0
    length = piece * groups
    width = H // groups * HD
    repeat = groups // KV
    own_rows = w_query.shape[0]

    chips = groups // 2
    half = chips // 2
    order = list(range(half)) + list(range(chips - 1, half - 1, -1))
    place = np.argsort(order)
    follow = [order[(place[c] + 1) % chips] for c in range(chips)]
    ring = [(2 * c + k, 2 * follow[c] + k) for c in range(chips) for k in range(2)]
    swap = [(i, i ^ 1) for i in range(groups)]

    seq_at = lax.axis_index("seq")
    core_at = seq_at % 2
    ring_at = jnp.asarray(place, jnp.int32)[seq_at // 2]
    chunk = [jnp.asarray(order, jnp.int32)[(ring_at + (chips - s)) % chips] for s in range(chips)]
    mine_at = [(2 * c + core_at) * piece for c in chunk]
    other_at = [(2 * c + 1 - core_at) * piece for c in chunk]
    dp_at = lax.axis_index("dp")

    def step_ring(x):
        return lax.ppermute(x, "seq", ring)

    def step_swap(x):
        return lax.ppermute(x, "seq", swap)

    def ring_gather(x):
        mine, other = [x], [step_swap(x)]
        for _ in range(chips - 1):
            mine.append(step_ring(mine[-1]))
            other.append(step_swap(mine[-1]))
        return mine, other

    def rows_at(x, start, count):
        return lax.dynamic_slice_in_dim(x, start, count, 0)

    x_own = tokens.reshape(piece, depth)
    cot_own = cotangent.reshape(piece, depth)

    def per_group(w):
        return jnp.repeat(w.reshape(own_rows, KV, HD), repeat, axis=1)

    gains_own = jnp.stack([gain_attn, gain_mlp], axis=-1)
    gains_own = jnp.pad(gains_own, ((0, 0), (0, LANES - 2)))
    gains_own = jnp.broadcast_to(gains_own[:, None, :], (own_rows, groups, LANES))
    own_cols = jnp.concatenate(
        [w_query.reshape(own_rows, groups, width), per_group(w_key), per_group(w_value), gains_own], axis=-1
    )
    cols = own_cols.shape[-1]
    cols_dp = lax.all_to_all(jnp.transpose(own_cols, (1, 0, 2)), "seq", 0, 0, tiled=True)
    dp_rows = groups * own_rows
    cols_dp = cols_dp.reshape(dp_rows, cols)
    cols_all = jnp.zeros((depth, cols), bf16)
    for k in range(dp_count):
        block = cols_dp if k == 0 else lax.ppermute(cols_dp, "dp", [(i, i ^ k) for i in range(dp_count)])
        cols_all = lax.dynamic_update_slice_in_dim(cols_all, block, (dp_at ^ k) * dp_rows, 0)
    w_qkv = cols_all[:, : width + 2 * HD]
    gains = jnp.transpose(cols_all[:, width + 2 * HD : width + 2 * HD + 2].astype(f32))
    gain_one, gain_two = gains[:1], gains[1:]

    out_full = lax.all_gather(w_out, ("dp", "seq"), axis=0, tiled=True)
    gate_full = lax.all_gather(w_gate, "dp", axis=0, tiled=True)
    up_full = lax.all_gather(w_up, "dp", axis=0, tiled=True)
    down_full = lax.all_gather(w_down, "dp", axis=0, tiled=True)

    cos, sin = rope_tables(length)

    x_mine, x_other = ring_gather(x_own)
    queries = jnp.zeros((length, width), bf16)
    keys_values = jnp.zeros((length, 2 * HD), bf16)
    normed_parts = []
    for s in range(chips):
        cos_s = jnp.concatenate([rows_at(cos, mine_at[s], piece), rows_at(cos, other_at[s], piece)], axis=0)
        sin_s = jnp.concatenate([rows_at(sin, mine_at[s], piece), rows_at(sin, other_at[s], piece)], axis=0)
        normed, qkv = qkv_call(x_mine[s], x_other[s], gain_one, w_qkv, cos_s, sin_s, width)
        normed_parts.append(normed)
        for start, part in ((mine_at[s], qkv[:piece]), (other_at[s], qkv[piece:])):
            queries = lax.dynamic_update_slice_in_dim(queries, part[:, :width], start, 0)
            keys_values = lax.dynamic_update_slice_in_dim(keys_values, part[:, width:], start, 0)

    c_mine, c_other = ring_gather(after(cot_own, x_mine[-1]))

    head_out, out_t, lse = attn_fwd(queries, keys_values)
    mixed = lax.all_to_all(head_out.reshape(groups, piece, width), "seq", 0, 0, tiled=True)
    middle, normed_two = out_call(mixed, out_full, x_own, gain_two)

    n_mine, n_other = ring_gather(normed_two)
    ffn = [
        ffn_call(n_mine[s], n_other[s], c_mine[s], c_other[s], gate_full, up_full, down_full)
        for s in range(chips)
    ]

    def ring_scatter(mine, other):
        got = [step_swap(o) for o in other]

        def own(s):
            return mine[s].astype(f32) + got[s].astype(f32)

        acc = own(1).astype(bf16)
        for s in range(2, chips):
            acc = (step_ring(acc).astype(f32) + own(s)).astype(bf16)
        return step_ring(acc), own(0)

    back_got, back_own = ring_scatter([f[3] for f in ffn], [f[4] for f in ffn])
    d_middle, branch, d_gain_two, d_mixed = mid_call(
        back_got, back_own, middle, cot_own, gain_two, out_full, width
    )
    down_got, down_own = ring_scatter(
        [after(f[5], back_got) for f in ffn], [after(f[6], back_got) for f in ffn]
    )
    block_out = (middle + (down_got.astype(f32) + down_own)).astype(bf16)

    n_all = jnp.concatenate([b for pair in zip(n_mine, n_other) for b in pair], axis=0)
    c_all = jnp.concatenate([b for pair in zip(c_mine, c_other) for b in pair], axis=0)

    def weight_grad(rows, grads):
        return mm(rows, jnp.concatenate(grads, axis=0), TN).astype(bf16)

    def scatter_dp(x):
        return lax.psum_scatter(x, "dp", scatter_dimension=0, tiled=True)

    grad_gate = scatter_dp(weight_grad(n_all, [f[1] for f in ffn])).astype(f32)
    grad_up = scatter_dp(weight_grad(n_all, [f[2] for f in ffn])).astype(f32)
    grad_down = scatter_dp(weight_grad(c_all, [f[0] for f in ffn])).astype(f32)

    grad_out = jnp.einsum("gnh,nd->ghd", mixed, branch, preferred_element_type=f32)
    grad_out = scatter_dp(grad_out.reshape(groups * width, depth).astype(bf16))
    grad_out = lax.psum_scatter(grad_out, "seq", scatter_dimension=0, tiled=True).astype(f32)

    d_heads = lax.all_to_all(d_mixed, "seq", 0, 0, tiled=True).reshape(length, width)
    d_queries, d_kv = attn_bwd(queries, keys_values, d_heads, out_t, lse, cos, sin)
    d_qkv = jnp.concatenate([d_queries, d_kv], axis=1)
    d_parts = [
        jnp.concatenate([rows_at(d_qkv, mine_at[s], piece), rows_at(d_qkv, other_at[s], piece)], axis=0)
        for s in range(chips)
    ]
    d_normed = [mm(part, w_qkv, NT).astype(bf16) for part in d_parts]
    first_got, first_own = ring_scatter([d[:piece] for d in d_normed], [d[piece:] for d in d_normed])
    grad_tokens = first_call(first_got, first_own, x_own, d_middle, gain_one)

    grad_cols = mm(jnp.concatenate(normed_parts, axis=0), jnp.concatenate(d_parts, axis=0), TN)
    high = d_gain_two.astype(bf16)
    rest = (d_gain_two - high.astype(f32)).astype(bf16)
    extra = jnp.pad(jnp.transpose(jnp.concatenate([high, rest], axis=0)), ((0, 0), (0, LANES - 2)))
    grad_cols = jnp.concatenate([grad_cols.astype(bf16), extra], axis=1)
    total = rows_at(grad_cols, dp_at * dp_rows, dp_rows).astype(f32)
    for k in range(1, dp_count):
        send = rows_at(grad_cols, (dp_at ^ k) * dp_rows, dp_rows)
        total = total + lax.ppermute(send, "dp", [(i, i ^ k) for i in range(dp_count)]).astype(f32)
    dealt = lax.all_to_all(
        total.astype(bf16).reshape(groups, own_rows, cols), "seq", 0, 0, tiled=True
    ).astype(f32)

    def join(x):
        return jnp.transpose(x, (1, 0, 2)).reshape(own_rows, -1)

    def fold(x):
        return join(jnp.sum(x.reshape(KV, repeat, own_rows, HD), axis=1))

    grad_query = join(dealt[:, :, :width])
    grad_key = fold(dealt[:, :, width : width + HD])
    grad_value = fold(dealt[:, :, width + HD : width + 2 * HD])
    grad_gain_two = jnp.sum(dealt[:, :, width + 2 * HD : width + 2 * HD + 2], axis=(0, 2))

    def against(w, grad):
        return jnp.sum(w.astype(f32) * grad, axis=1)

    grad_gain_one = against(w_query, grad_query) + against(w_key, grad_key) + against(w_value, grad_value)
    grad_gain_one = grad_gain_one / gain_attn.astype(f32)

    return (
        block_out.reshape(1, piece, depth),
        grad_tokens.reshape(1, piece, depth),
        grad_gain_one,
        grad_query,
        grad_key,
        grad_value,
        grad_out,
        grad_gain_two,
        grad_gate,
        grad_up,
        grad_down,
    )


def solution(mesh):
    rows = P("dp", "seq", None)
    both = P(("dp", "seq"))
    flat = P(("dp", "seq"), None)
    tiles = P("dp", "seq")
    in_specs = (rows, both, flat, flat, flat, flat, both, tiles, tiles, tiles, rows)
    out_specs = (rows, rows, both, flat, flat, flat, flat, both, tiles, tiles, tiles)
    return jax.shard_map(shards, mesh=mesh, in_specs=in_specs, out_specs=out_specs, check_vma=False)
```

```python
import functools

import jax
import jax.numpy as jnp
import numpy as np
from jax import lax
from jax.experimental import pallas as pl
from jax.experimental.pallas import tpu as pltpu
from jax.sharding import PartitionSpec as P

H = 32
KV = 8
HD = 64
LANES = 128
VMEM_BYTES = 50 * 2**20

epsilon = 1e-05
rope_theta = 500000.0
rope_factor = 32.0
old_context = 8192.0

f32 = jnp.float32
bf16 = jnp.bfloat16

NN = (((1,), (0,)), ((), ()))
NT = (((1,), (1,)), ((), ()))
TN = (((0,), (0,)), ((), ()))


def mm(a, b, dims):
    return lax.dot_general(a, b, dims, preferred_element_type=f32)


def cost(flops, moved, transcendentals=0):
    return pl.CostEstimate(flops=flops, bytes_accessed=moved, transcendentals=transcendentals)


def params():
    return pltpu.CompilerParams(vmem_limit_bytes=VMEM_BYTES)


def frequencies(head_size):
    halves = jnp.arange(head_size // 2).astype(f32)
    plain = rope_theta ** (-2.0 * halves / head_size)
    blend = jnp.clip((old_context * plain / (2.0 * jnp.pi) - 1.0) / 3.0, 0.0, 1.0)
    return (1.0 - blend) * plain / rope_factor + blend * plain


def rope_tables(length):
    freq = jnp.tile(frequencies(HD), LANES // (HD // 2))
    angles = jnp.arange(length).astype(f32)[:, None] * freq[None, :]
    sign = jnp.where((jnp.arange(LANES) % HD) < HD // 2, -1.0, 1.0).astype(f32)
    return jnp.cos(angles), jnp.sin(angles) * sign[None, :]


def turn(x, cos, sin):
    lane = lax.broadcasted_iota(jnp.int32, x.shape, 1)
    swapped = jnp.where(
        lane % HD < HD // 2, pltpu.roll(x, LANES - HD // 2, 1), pltpu.roll(x, HD // 2, 1)
    )
    return x * cos + swapped * sin


def qkv_kernel(width, at, mine, other, gain, w, cos, sin, *refs):
    normed, queries, keys_values = refs[-3:]
    x = jnp.where(pl.program_id(0) == 0, mine[...], other[...]).astype(f32)
    inverse = lax.rsqrt(jnp.mean(x * x, axis=-1, keepdims=True) + epsilon)
    low = (x * inverse * gain[...]).astype(bf16)
    normed[...] = low
    y = mm(low, w[...], NN)
    for first in range(0, width, LANES):
        part = y[:, first : first + LANES]
        queries[:, first : first + LANES] = turn(part, cos[...], sin[...]).astype(bf16)
    part = y[:, width : width + LANES]
    lane = lax.broadcasted_iota(jnp.int32, part.shape, 1)
    keys_values[...] = jnp.where(lane < HD, turn(part, cos[...], sin[...]), part).astype(bf16)


def qkv_call(at, mine, other, gain, w, cos, sin, width, length, held):
    rows, depth = mine.shape
    cols = w.shape[1]

    def whole(shape):
        return pl.BlockSpec(shape, lambda i, at: (0, 0))

    def placed(n):
        return pl.BlockSpec((rows, n), lambda i, at: (at[i], 0))

    return pl.pallas_call(
        functools.partial(qkv_kernel, width),
        grid_spec=pltpu.PrefetchScalarGridSpec(
            num_scalar_prefetch=1,
            grid=(2,),
            in_specs=[
                whole((rows, depth)),
                whole((rows, depth)),
                whole((1, depth)),
                whole((depth, cols)),
                placed(LANES),
                placed(LANES),
            ]
            + [pl.BlockSpec(memory_space=pl.ANY)] * len(held),
            out_specs=[placed(depth), placed(width), placed(2 * HD)],
        ),
        out_shape=[
            jax.ShapeDtypeStruct((length, depth), bf16),
            jax.ShapeDtypeStruct((length, width), bf16),
            jax.ShapeDtypeStruct((length, 2 * HD), bf16),
        ],
        input_output_aliases={7 + i: i for i in range(len(held))},
        compiler_params=params(),
        cost_estimate=cost(4 * rows * depth * cols, 8 * rows * depth + 2 * depth * cols),
        name="qkv",
    )(at, mine, other, gain, w, cos, sin, *held)


def fwd_kernel(bq, share, q_ref, kv_ref, out_ref, ot_ref, lse_ref, m_s, l_s, acc_s):
    i = pl.program_id(0)
    m_s[...] = jnp.full(m_s.shape, -1e30, f32)
    l_s[...] = jnp.zeros(l_s.shape, f32)
    acc_s[...] = jnp.zeros(acc_s.shape, f32)
    qs = q_ref[...] * jnp.asarray(HD**-0.5, bf16)

    def step(j, masked):
        start = pl.multiple_of(j * bq, bq)
        kk = kv_ref[pl.ds(start, bq), :HD]
        vv = kv_ref[pl.ds(start, bq), HD:]
        for h in range(share):
            at = slice(h * HD, (h + 1) * HD)
            s = mm(kk, qs[:, at], NT)
            if masked:
                ki = lax.broadcasted_iota(jnp.int32, s.shape, 0)
                qi = lax.broadcasted_iota(jnp.int32, s.shape, 1)
                s = jnp.where(ki <= qi, s, -1e30)
            m_old = m_s[h : h + 1, :]
            m_new = jnp.maximum(m_old, jnp.max(s, axis=0, keepdims=True))
            p = jnp.exp(s - m_new)
            alpha = jnp.exp(m_old - m_new)
            l_s[h : h + 1, :] = l_s[h : h + 1, :] * alpha + jnp.sum(p, axis=0, keepdims=True)
            m_s[h : h + 1, :] = m_new
            acc_s[at, :] = acc_s[at, :] * alpha + mm(vv, p.astype(bf16), TN)

    def plain(j, carry):
        step(j, False)
        return carry

    lax.fori_loop(0, i, plain, 0)
    step(i, True)
    for h in range(share):
        at = slice(h * HD, (h + 1) * HD)
        total = l_s[h : h + 1, :]
        ot_ref[at, :] = acc_s[at, :] / total
        lse_ref[h : h + 1, :] = m_s[h : h + 1, :] + jnp.log(total)
    out_ref[...] = ot_ref[...].T.astype(bf16)


def attn_fwd(q, kv, bq=1024):
    length, width = q.shape
    share = width // HD
    rows = max(8, share)
    return pl.pallas_call(
        functools.partial(fwd_kernel, bq, share),
        grid=(length // bq,),
        in_specs=[
            pl.BlockSpec((bq, width), lambda i: (i, 0)),
            pl.BlockSpec((length, 2 * HD), lambda i: (0, 0)),
        ],
        out_specs=[
            pl.BlockSpec((bq, width), lambda i: (i, 0)),
            pl.BlockSpec((width, bq), lambda i: (0, i)),
            pl.BlockSpec((rows, bq), lambda i: (0, i)),
        ],
        out_shape=[
            jax.ShapeDtypeStruct((length, width), bf16),
            jax.ShapeDtypeStruct((width, length), f32),
            jax.ShapeDtypeStruct((rows, length), f32),
        ],
        scratch_shapes=[
            pltpu.VMEM((rows, bq), f32),
            pltpu.VMEM((rows, bq), f32),
            pltpu.VMEM((width, bq), f32),
        ],
        compiler_params=params(),
        cost_estimate=cost(8 * length * length * width, 8 * length * width, share * length * length // 2),
        name="attn_fwd",
    )(q, kv)


def bwd_kernel(
    bq, share, q_ref, kv_ref, do_ref, ot_ref, lse_ref, cos_ref, sin_ref, dq_ref, dkv_ref, dqt_s, dk_s, dv_s
):
    i = pl.program_id(0)

    @pl.when(i == 0)
    def _():
        dk_s[...] = jnp.zeros(dk_s.shape, f32)
        dv_s[...] = jnp.zeros(dv_s.shape, f32)

    dqt_s[...] = jnp.zeros(dqt_s.shape, f32)
    qs = q_ref[...] * jnp.asarray(HD**-0.5, bf16)
    do = do_ref[...]
    product = do.astype(f32).T * ot_ref[...]
    inner = [jnp.sum(product[h * HD : (h + 1) * HD], axis=0, keepdims=True) for h in range(share)]

    def step(j, masked):
        start = pl.multiple_of(j * bq, bq)
        kk = kv_ref[pl.ds(start, bq), :HD]
        vv = kv_ref[pl.ds(start, bq), HD:]
        dk = jnp.zeros((bq, HD), f32)
        dv = jnp.zeros((bq, HD), f32)
        for h in range(share):
            at = slice(h * HD, (h + 1) * HD)
            s = mm(kk, qs[:, at], NT)
            p = jnp.exp(s - lse_ref[h : h + 1, :])
            if masked:
                ki = lax.broadcasted_iota(jnp.int32, s.shape, 0)
                qi = lax.broadcasted_iota(jnp.int32, s.shape, 1)
                p = jnp.where(ki <= qi, p, 0.0)
            dp = mm(vv, do[:, at], NT)
            ds = (p * (dp - inner[h])).astype(bf16)
            dv = dv + mm(p.astype(bf16), do[:, at], NN)
            dk = dk + mm(ds, qs[:, at], NN)
            dqt_s[at, :] += mm(kk, ds, TN)
        dk_s[pl.ds(start, bq), :] += dk
        dv_s[pl.ds(start, bq), :] += dv

    def plain(j, carry):
        step(j, False)
        return carry

    lax.fori_loop(0, i, plain, 0)
    step(i, True)
    dq = (dqt_s[...] * (HD**-0.5)).T.astype(bf16).astype(f32)
    rows = pl.ds(pl.multiple_of(i * bq, bq), bq)
    for at in range(0, share * HD, LANES):
        part = dq[:, at : at + LANES]
        dq_ref[:, at : at + LANES] = turn(part, cos_ref[rows, :], -sin_ref[rows, :]).astype(bf16)

    @pl.when(i == pl.num_programs(0) - 1)
    def _():
        both = jnp.concatenate([dk_s[...], dv_s[...]], axis=1).astype(bf16).astype(f32)
        lane = lax.broadcasted_iota(jnp.int32, both.shape, 1)
        turned = turn(both, cos_ref[...], -sin_ref[...])
        dkv_ref[...] = jnp.where(lane < HD, turned, both).astype(bf16)


def attn_bwd(q, kv, do, ot, lse, cos, sin, bq=512):
    length, width = q.shape
    share = width // HD
    rows = lse.shape[0]
    return pl.pallas_call(
        functools.partial(bwd_kernel, bq, share),
        grid=(length // bq,),
        in_specs=[
            pl.BlockSpec((bq, width), lambda i: (i, 0)),
            pl.BlockSpec((length, 2 * HD), lambda i: (0, 0)),
            pl.BlockSpec((bq, width), lambda i: (i, 0)),
            pl.BlockSpec((width, bq), lambda i: (0, i)),
            pl.BlockSpec((rows, bq), lambda i: (0, i)),
            pl.BlockSpec((length, LANES), lambda i: (0, 0)),
            pl.BlockSpec((length, LANES), lambda i: (0, 0)),
        ],
        out_specs=[
            pl.BlockSpec((bq, width), lambda i: (i, 0)),
            pl.BlockSpec((length, 2 * HD), lambda i: (0, 0)),
        ],
        out_shape=[
            jax.ShapeDtypeStruct((length, width), bf16),
            jax.ShapeDtypeStruct((length, 2 * HD), bf16),
        ],
        scratch_shapes=[
            pltpu.VMEM((width, bq), f32),
            pltpu.VMEM((length, HD), f32),
            pltpu.VMEM((length, HD), f32),
        ],
        compiler_params=params(),
        cost_estimate=cost(20 * length * length * width, 16 * length * width, share * length * length // 2),
        name="attn_bwd",
    )(q, kv, do, ot, lse, cos, sin)


def out_kernel(pieces, blocks, at, *refs):
    w_mine, w_other = refs[:pieces], refs[pieces : 2 * pieces]
    mixed, x, gain, middle, normed, acc = refs[2 * pieces :]
    groups = mixed.shape[0]
    depth = x.shape[1]
    half, block, tile = depth // 2, depth // blocks, w_mine[0].shape[1]
    steps = half // tile
    u = pl.program_id(0)
    heads = jnp.concatenate([mixed[at[1 + blocks + g]] for g in range(groups)], axis=1)

    def put(ws, first):
        w = jnp.concatenate([r[...] for r in ws], axis=0)
        acc[:, pl.ds(pl.multiple_of(first, LANES), tile)] = mm(heads, w, NN)

    @pl.when(u < steps)
    def _():
        put(w_mine, at[0] * half + u * tile)

    @pl.when(u >= steps)
    def _():
        put(w_other, (1 - at[0]) * half + (u - steps) * tile)

    @pl.when(u == pl.num_programs(0) - 1)
    def _():
        squares = jnp.zeros((x.shape[0], 1), f32)
        for k in range(blocks):
            here = slice(k * block, (k + 1) * block)
            total = acc[:, pl.ds(pl.multiple_of(at[1 + k] * block, LANES), block)] + x[:, here].astype(f32)
            middle[:, here] = total
            squares = squares + jnp.sum(total * total, axis=-1, keepdims=True)
        inverse = lax.rsqrt(squares / depth + epsilon)
        normed[...] = (middle[...] * inverse * gain[...]).astype(bf16)


def halves_specs(w, tile, steps):
    mine = [pl.BlockSpec((p.shape[0], tile), lambda u, at: (0, jnp.minimum(u, steps - 1))) for p in w]
    other = [pl.BlockSpec((p.shape[0], tile), lambda u, at: (0, jnp.maximum(u - steps, 0))) for p in w]
    return mine + other


def out_call(at, w_mine, w_other, mixed, x, gain, blocks, tile=512):
    groups, rows, part = mixed.shape
    depth = x.shape[1]
    steps = depth // 2 // tile

    def whole(shape):
        return pl.BlockSpec(shape, lambda u, at: (0,) * len(shape))

    return pl.pallas_call(
        functools.partial(out_kernel, len(w_mine), blocks),
        grid_spec=pltpu.PrefetchScalarGridSpec(
            num_scalar_prefetch=1,
            grid=(2 * steps,),
            in_specs=halves_specs(w_mine, tile, steps)
            + [whole(mixed.shape), whole(x.shape), whole((1, depth))],
            out_specs=[whole((rows, depth)), whole((rows, depth))],
            scratch_shapes=[pltpu.VMEM((rows, depth), f32)],
        ),
        out_shape=[
            jax.ShapeDtypeStruct((rows, depth), f32),
            jax.ShapeDtypeStruct((rows, depth), bf16),
        ],
        compiler_params=params(),
        cost_estimate=cost(2 * groups * part * rows * depth, 2 * groups * part * depth + 8 * rows * depth),
        name="out_norm",
    )(at, *w_mine, *w_other, mixed, x, gain)


def ffn_kernel(pieces, *refs):
    x_mine, x_other, c_mine, c_other = refs[:4]
    weights = [refs[4 + i * pieces : 4 + (i + 1) * pieces] for i in range(3)]
    xs, cs, hidden, d_gate, d_up, back_mine, down_mine, others, back, down = refs[-10:]
    u = pl.program_id(0)
    w_gate, w_up, w_down = (jnp.concatenate([r[...] for r in w], axis=0) for w in weights)
    x = jnp.concatenate([x_mine[...], x_other[...]], axis=0)
    c = jnp.concatenate([c_mine[...], c_other[...]], axis=0)
    gate = mm(x, w_gate, NN)
    up = mm(x, w_up, NN)
    grad = mm(c, w_down, NN)
    sig = jax.nn.sigmoid(gate)
    silu = gate * sig
    act = (silu * up).astype(bf16)
    dg = (grad * up * sig * (1.0 + gate * (1.0 - sig))).astype(bf16)
    du = (grad * silu).astype(bf16)
    hidden[...] = act
    d_gate[...] = dg
    d_up[...] = du

    @pl.when(u == 0)
    def _():
        xs[...] = x
        cs[...] = c
        back[...] = mm(dg, w_gate, NT) + mm(du, w_up, NT)
        down[...] = mm(act, w_down, NT)

    @pl.when(u > 0)
    def _():
        back[...] += mm(dg, w_gate, NT) + mm(du, w_up, NT)
        down[...] += mm(act, w_down, NT)

    @pl.when(u == pl.num_programs(0) - 1)
    def _():
        rows = back_mine.shape[0]
        back_mine[...] = back[:rows].astype(bf16)
        down_mine[...] = down[:rows].astype(bf16)
        others[0] = back[rows:].astype(bf16)
        others[1] = down[rows:].astype(bf16)


def ffn_call(s, count, x_mine, x_other, c_mine, c_other, w_gate, w_up, w_down, held, tile=256):
    rows, depth = x_mine.shape
    units = w_gate[0].shape[1]
    block = pl.BlockSpec((rows, depth), lambda u: (0, 0))
    weights = [pl.BlockSpec((p.shape[0], tile), lambda u: (0, u)) for p in w_gate]
    full = pl.BlockSpec((2 * rows, depth), lambda u: (s, 0))
    act = pl.BlockSpec((2 * rows, tile), lambda u: (s, u))
    full_shape = jax.ShapeDtypeStruct((2 * rows * count, depth), bf16)
    act_shape = jax.ShapeDtypeStruct((2 * rows * count, units), bf16)
    row_shape = jax.ShapeDtypeStruct((rows, depth), bf16)
    first = 4 + 3 * len(w_gate)
    return pl.pallas_call(
        functools.partial(ffn_kernel, len(w_gate)),
        grid=(units // tile,),
        in_specs=[block] * 4 + weights * 3 + [pl.BlockSpec(memory_space=pl.ANY)] * len(held),
        out_specs=[full] * 2 + [act] * 3 + [block] * 2 + [pl.BlockSpec((2, rows, depth), lambda u: (0, 0, 0))],
        out_shape=[full_shape] * 2
        + [act_shape] * 3
        + [row_shape] * 2
        + [jax.ShapeDtypeStruct((2, rows, depth), bf16)],
        scratch_shapes=[pltpu.VMEM((2 * rows, depth), f32)] * 2,
        input_output_aliases={first + i: i for i in range(len(held))},
        compiler_params=params(),
        cost_estimate=cost(24 * rows * depth * units, 6 * depth * units + 20 * rows * depth + 12 * rows * units),
        name="ffn",
    )(x_mine, x_other, c_mine, c_other, *w_gate, *w_up, *w_down, *held)


def mid_kernel(pieces, blocks, at, *refs):
    w_mine, w_other = refs[:pieces], refs[pieces : 2 * pieces]
    ring, own, swapped, middle, cot, gain, d_middle, branch, d_gain, d_mixed, acc = refs[2 * pieces :]
    rows, depth = middle.shape
    groups, _, part = d_mixed.shape
    half, block, tile = depth // 2, depth // blocks, w_mine[0].shape[1]
    steps = half // tile
    u = pl.program_id(0)

    @pl.when(u == 0)
    def _():
        grad = ring[...].astype(f32) + (own[...].astype(f32) + swapped[...].astype(f32))
        m = middle[...]
        inverse = lax.rsqrt(jnp.mean(m * m, axis=-1, keepdims=True) + epsilon)
        scaled = grad * gain[...]
        slope = jnp.mean(m * scaled, axis=-1, keepdims=True) * (inverse * inverse * inverse)
        total = cot[...].astype(f32) + inverse * scaled - m * slope
        d_middle[...] = total
        for k in range(blocks):
            place = pl.ds(pl.multiple_of(at[1 + k] * block, LANES), block)
            branch[:, place] = total[:, k * block : (k + 1) * block].astype(bf16)
        d_gain[...] = jnp.sum(grad * m * inverse, axis=0, keepdims=True)
        acc[...] = jnp.zeros(acc.shape, f32)

    def add(ws, first):
        w = jnp.concatenate([r[...] for r in ws], axis=0)
        acc[...] += mm(branch[:, pl.ds(pl.multiple_of(first, LANES), tile)], w, NT)

    @pl.when(u < steps)
    def _():
        add(w_mine, at[0] * half + u * tile)

    @pl.when(u >= steps)
    def _():
        add(w_other, (1 - at[0]) * half + (u - steps) * tile)

    @pl.when(u == pl.num_programs(0) - 1)
    def _():
        for g in range(groups):
            d_mixed[at[1 + blocks + g]] = acc[:, g * part : (g + 1) * part].astype(bf16)


def mid_call(at, w_mine, w_other, ring, own, swapped, middle, cot, gain, part, blocks, tile=512):
    rows, depth = middle.shape
    heads = sum(p.shape[0] for p in w_mine)
    groups = heads // part
    steps = depth // 2 // tile

    def whole(shape):
        return pl.BlockSpec(shape, lambda u, at: (0,) * len(shape))

    block, line = whole((rows, depth)), whole((1, depth))
    return pl.pallas_call(
        functools.partial(mid_kernel, len(w_mine), blocks),
        grid_spec=pltpu.PrefetchScalarGridSpec(
            num_scalar_prefetch=1,
            grid=(2 * steps,),
            in_specs=halves_specs(w_mine, tile, steps) + [block] * 5 + [line],
            out_specs=[block, block, line, whole((groups, rows, part))],
            scratch_shapes=[pltpu.VMEM((rows, heads), f32)],
        ),
        out_shape=[
            jax.ShapeDtypeStruct((rows, depth), f32),
            jax.ShapeDtypeStruct((rows, depth), bf16),
            jax.ShapeDtypeStruct((1, depth), f32),
            jax.ShapeDtypeStruct((groups, rows, part), bf16),
        ],
        compiler_params=params(),
        cost_estimate=cost(2 * heads * rows * depth, 2 * heads * depth + 16 * rows * depth),
        name="mid",
    )(at, *w_mine, *w_other, ring, own, swapped, middle, cot, gain)


def first_kernel(blocks, at, ring, own, swapped, x_ref, d_middle, gain, out):
    depth = x_ref.shape[1]
    block = depth // blocks
    grad = ring[...].astype(f32) + (own[...].astype(f32) + swapped[...].astype(f32))
    x = x_ref[...].astype(f32)
    inverse = lax.rsqrt(jnp.mean(x * x, axis=-1, keepdims=True) + epsilon)
    scaled = grad * gain[...]
    slope = jnp.mean(x * scaled, axis=-1, keepdims=True) * (inverse * inverse * inverse)
    total = d_middle[...] + inverse * scaled - x * slope
    for k in range(blocks):
        place = pl.ds(pl.multiple_of(at[1 + k] * block, LANES), block)
        out[:, place] = total[:, k * block : (k + 1) * block].astype(bf16)


def first_call(at, ring, own, swapped, x, d_middle, gain, blocks, tile=64):
    rows, depth = x.shape
    block = pl.BlockSpec((tile, depth), lambda i, at: (i, 0))
    return pl.pallas_call(
        functools.partial(first_kernel, blocks),
        grid_spec=pltpu.PrefetchScalarGridSpec(
            num_scalar_prefetch=1,
            grid=(rows // tile,),
            in_specs=[block] * 5 + [pl.BlockSpec((1, depth), lambda i, at: (0, 0))],
            out_specs=block,
        ),
        out_shape=jax.ShapeDtypeStruct((rows, depth), bf16),
        compiler_params=params(),
        cost_estimate=cost(20 * rows * depth, 14 * rows * depth),
        name="first_norm_back",
    )(at, ring, own, swapped, x, d_middle, gain)


def after(value, *others):
    return lax.optimization_barrier((value,) + others)[0]


def shards(
    tokens, gain_attn, w_query, w_key, w_value, w_out, gain_mlp, w_gate, w_up, w_down, cotangent
):
    groups = lax.axis_size("seq")
    dp_count = lax.axis_size("dp")
    seq_count, piece, depth = tokens.shape
    assert seq_count == 1 and groups >= KV and groups % 2 == 0 and groups % dp_count == 0
    assert dp_count & (dp_count - 1) == 0
    length = piece * groups
    width = H // groups * HD
    repeat = groups // KV
    own_rows = w_query.shape[0]
    half = depth // 2
    block = depth // dp_count

    chips = groups // 2
    middle_chip = chips // 2
    order = list(range(middle_chip)) + list(range(chips - 1, middle_chip - 1, -1))
    place = np.argsort(order)
    follow = [order[(place[c] + 1) % chips] for c in range(chips)]
    ring = [(2 * c + k, 2 * follow[c] + k) for c in range(chips) for k in range(2)]
    swap = [(i, i ^ 1) for i in range(groups)]

    seq_at = lax.axis_index("seq")
    dp_at = lax.axis_index("dp")
    core_at = seq_at % 2
    ring_at = jnp.asarray(place, jnp.int32)[seq_at // 2]
    chunk = jnp.asarray(order, jnp.int32)[(ring_at + chips - jnp.arange(chips)) % chips]
    pair_at = 2 * chunk[:, None] + jnp.stack([core_at, 1 - core_at])[None, :]
    dp_order = dp_at ^ jnp.arange(dp_count)
    group_order = (dp_order[:, None] * (groups // dp_count) + jnp.arange(groups // dp_count)).reshape(-1)
    at = jnp.concatenate([core_at[None], dp_order, group_order]).astype(jnp.int32)

    def step_ring(x):
        return lax.ppermute(x, "seq", ring)

    def step_swap(x):
        return lax.ppermute(x, "seq", swap)

    def step_dp(x, k):
        return lax.ppermute(x, "dp", [(i, i ^ k) for i in range(dp_count)])

    def rows_at(x, start, count):
        return lax.dynamic_slice_in_dim(x, start, count, 0)

    def cols_at(x, start, count):
        return lax.dynamic_slice_in_dim(x, start, count, 1)

    def reorder(x):
        return jnp.concatenate([cols_at(x, dp_order[k] * block, block) for k in range(dp_count)], axis=1)

    def gather_dp(x):
        if dp_count != 4:
            return [x] + [step_dp(x, k) for k in range(1, dp_count)]
        cut = x.shape[0] // 2
        one, two = step_dp(x, 1), step_dp(x, 2)
        return [x, one, two, step_dp(one[:cut], 2), step_dp(two[cut:], 1)]

    def scatter_dp(parts):
        return [step_dp(parts[k], k) for k in range(1, dp_count)]

    def pair_sides(own, got):
        return jnp.where(core_at == 0, jnp.concatenate([own, got]), jnp.concatenate([got, own]))

    x_own = reorder(tokens.reshape(piece, depth))
    cot_own = reorder(cotangent.reshape(piece, depth))

    with jax.named_scope("tokens_ring"):
        x_mine, x_other = [x_own], [step_swap(x_own)]
        for _ in range(chips - 1):
            x_mine.append(step_ring(x_mine[-1]))
            x_other.append(step_swap(x_mine[-1]))

    def per_group(w):
        return jnp.repeat(w.reshape(own_rows, KV, HD), repeat, axis=1)

    with jax.named_scope("projection_columns"):
        gains_own = jnp.stack([gain_attn, gain_mlp], axis=-1)
        gains_own = jnp.pad(gains_own, ((0, 0), (0, LANES - 2)))
        gains_own = jnp.broadcast_to(gains_own[:, None, :], (own_rows, groups, LANES))
        own_cols = jnp.concatenate(
            [w_query.reshape(own_rows, groups, width), per_group(w_key), per_group(w_value), gains_own],
            axis=-1,
        )
        cols = own_cols.shape[-1]
        dp_rows = groups * own_rows
        cols_dp = lax.all_to_all(jnp.transpose(own_cols, (1, 0, 2)), "seq", 0, 0, tiled=True)
        cols_dp = cols_dp.reshape(dp_rows, cols)
        cols_all = jnp.concatenate([cols_dp] + [step_dp(cols_dp, k) for k in range(1, dp_count)], axis=0)
        w_qkv = cols_all[:, : width + 2 * HD]
        gains = jnp.transpose(cols_all[:, width + 2 * HD : width + 2 * HD + 2].astype(f32))
        gain_one, gain_two = gains[:1], gains[1:]

    with jax.named_scope("out_weight"):
        keep = cols_at(w_out, core_at * half, half)
        give = cols_at(w_out, (1 - core_at) * half, half)
        chip_rows = [pair_sides(keep, step_swap(give))]
        for _ in range(chips - 1):
            chip_rows.append(step_ring(chip_rows[-1]))
        out_rows = jnp.zeros((dp_rows, half), bf16)
        for s in range(chips):
            out_rows = lax.dynamic_update_slice_in_dim(out_rows, chip_rows[s], chunk[s] * 2 * own_rows, 0)

    with jax.named_scope("gate_weight"):
        gate_full = gather_dp(w_gate)
    with jax.named_scope("out_weight"):
        out_mine = gather_dp(after(out_rows, gate_full[-1]))
        out_other = [step_swap(p) for p in out_mine]
    with jax.named_scope("up_weight"):
        up_full = gather_dp(after(w_up, out_mine[-1]))
    with jax.named_scope("down_weight"):
        down_full = gather_dp(after(w_down, up_full[-1]))

    cos, sin = rope_tables(length)

    held = ()
    for s in range(chips):
        held = qkv_call(
            pair_at[s], x_mine[s], x_other[s], gain_one, w_qkv, cos, sin, width, length, held
        )
    normed, queries, keys_values = held

    with jax.named_scope("cotangent_ring"):
        c_mine = [cot_own, step_ring(after(cot_own, x_mine[-1]))]
        c_other = [step_swap(c) for c in c_mine]

    head_out, out_t, lse = attn_fwd(queries, keys_values)
    with jax.named_scope("mixed"):
        mixed = lax.all_to_all(head_out.reshape(groups, piece, width), "seq", 0, 0, tiled=True)
    middle, normed_two = out_call(at, out_mine, out_other, mixed, x_own, gain_two, dp_count)

    n_mine, n_other, ffn, held = [], [], [], ()
    for s in range(chips):
        with jax.named_scope("normed_ring"):
            n_mine.append(step_ring(n_mine[-1]) if s else normed_two)
            n_other.append(step_swap(n_mine[-1]))
        if s >= 2:
            with jax.named_scope("cotangent_ring"):
                c_mine.append(step_ring(after(c_mine[-1], mixed if s == 2 else n_mine[s - 2])))
                c_other.append(step_swap(c_mine[-1]))
        out = ffn_call(
            s, chips, n_mine[s], n_other[s], c_mine[s], c_other[s], gate_full, up_full, down_full, held
        )
        held, rest = out[:5], out[5:]
        with jax.named_scope("feed_forward_pair"):
            swapped = step_swap(rest[2])
        ffn.append((rest[0], rest[1], swapped[0], swapped[1]))
    n_all, c_all, hidden, d_gate, d_up = held

    def add(*parts):
        total = parts[0].astype(f32)
        for p in parts[1:]:
            total = total + p.astype(f32)
        return total

    def weight_grad(rows, grads):
        return [
            mm(rows[:, k * block : (k + 1) * block], grads, TN).astype(bf16) for k in range(dp_count)
        ]

    with jax.named_scope("back_ring"):
        acc = add(ffn[1][0], ffn[1][2]).astype(bf16)
        for s in range(2, chips):
            acc = add(step_ring(acc), ffn[s][0], ffn[s][2]).astype(bf16)
        back_got = step_ring(acc)

    with jax.named_scope("gate_grad"):
        gate_parts = weight_grad(n_all, d_gate)
        gate_sent = scatter_dp(gate_parts)
    with jax.named_scope("up_grad"):
        up_parts = weight_grad(n_all, d_up)
        up_sent = scatter_dp([after(p, gate_sent[-1]) for p in up_parts])
    back_got = after(back_got, gate_parts[-1], up_parts[-1])

    d_middle, branch, d_gain_two, d_mixed = mid_call(
        at, out_mine, out_other, back_got, ffn[0][0], ffn[0][2], middle, cot_own, gain_two, width, dp_count
    )
    with jax.named_scope("d_mixed"):
        d_heads = lax.all_to_all(d_mixed, "seq", 0, 0, tiled=True).reshape(length, width)

    with jax.named_scope("out_grad"):

        def out_part(start):
            g = jnp.einsum("gnh,nd->ghd", mixed, cols_at(branch, start, half), preferred_element_type=f32)
            return g.reshape(groups * width, half).astype(bf16)

        out_theirs = out_part((1 - core_at) * half)
        out_theirs_sent = step_swap(out_theirs)
        out_own = out_part(core_at * half)
    with jax.named_scope("down_grad"):
        down_rows, _ = lax.optimization_barrier((c_all, branch))
        down_parts = weight_grad(down_rows, hidden)
        down_sent = scatter_dp([after(p, up_sent[-1]) for p in down_parts])

    with jax.named_scope("down_ring"):
        acc = add(after(ffn[1][1], back_got), ffn[1][3]).astype(bf16)
        down_two = step_ring(acc)

    d_heads = after(d_heads, down_parts[-1], out_own)

    d_queries, d_kv = attn_bwd(queries, keys_values, d_heads, out_t, lse, cos, sin)

    with jax.named_scope("down_ring"):
        for s in range(2, chips):
            acc = add(after(down_two, d_heads if s == 2 else d_kv), ffn[s][1], ffn[s][3]).astype(bf16)
            down_two = step_ring(acc)

    with jax.named_scope("out_grad"):
        out_sum = add(out_own, after(out_theirs_sent, d_kv)).astype(bf16)
        out_parts = [rows_at(out_sum, dp_order[k] * dp_rows, dp_rows) for k in range(dp_count)]
        out_sent = scatter_dp([after(p, down_sent[-1]) for p in out_parts])

    with jax.named_scope("first_ring"):
        def d_normed(s, side):
            d_q = rows_at(d_queries, pair_at[s, side] * piece, piece)
            d_k = rows_at(d_kv, pair_at[s, side] * piece, piece)
            return mm(jnp.concatenate([d_q, d_k], axis=1), w_qkv, NT).astype(bf16)

        steps = list(range(1, chips)) + [0]
        theirs = {s: step_swap(d_normed(s, 1)) for s in steps}
        own = {s: d_normed(s, 0) for s in steps}
        acc = add(own[1], theirs[1]).astype(bf16)
        for s in range(2, chips):
            acc = add(step_ring(acc), own[s], theirs[s]).astype(bf16)
        first_last = acc
        first_got = step_ring(acc)

    with jax.named_scope("projection_grads"):
        d_qkv = jnp.concatenate([d_queries, d_kv], axis=1)
        grad_cols = mm(normed, d_qkv, TN).astype(bf16)
        high = d_gain_two.astype(bf16)
        rest = (d_gain_two - high.astype(f32)).astype(bf16)
        extra = jnp.pad(jnp.transpose(jnp.concatenate([high, rest], axis=0)), ((0, 0), (0, LANES - 2)))
        grad_cols = jnp.concatenate([grad_cols, extra], axis=1)
        col_parts = [grad_cols[k * block : (k + 1) * block] for k in range(dp_count)]
        total = add(col_parts[0], *scatter_dp(col_parts)).astype(bf16)
        dealt = lax.all_to_all(total.reshape(groups, own_rows, cols), "seq", 0, 0, tiled=True)

    with jax.named_scope("feed_forward_grads"):
        gate_sent, up_sent, down_sent = lax.optimization_barrier((gate_sent, up_sent, down_sent, first_last))[:3]
        grad_gate = add(gate_parts[0], *gate_sent)
        grad_up = add(up_parts[0], *up_sent)
        grad_down = add(down_parts[0], *down_sent)

    with jax.named_scope("out_grad"):
        out_dp = add(out_parts[0], *out_sent).astype(bf16)

        def chip_part(s):
            return rows_at(out_dp, chunk[s] * 2 * own_rows, 2 * own_rows)

        acc = chip_part(1)
        for s in range(2, chips):
            acc = add(step_ring(acc), chip_part(s)).astype(bf16)
        acc = add(step_ring(acc), chip_part(0))
        out_keep = rows_at(acc, core_at * own_rows, own_rows)
        out_give = rows_at(acc, (1 - core_at) * own_rows, own_rows).astype(bf16)
        out_take = step_swap(out_give).astype(f32)
        grad_out = jnp.where(
            core_at == 0,
            jnp.concatenate([out_keep, out_take], axis=1),
            jnp.concatenate([out_take, out_keep], axis=1),
        )

    grad_tokens = first_call(at, first_got, own[0], theirs[0], x_own, d_middle, gain_one, dp_count)
    block_out = reorder((middle + add(down_two, ffn[0][1], ffn[0][3])).astype(bf16))

    def join(x):
        return jnp.transpose(x, (1, 0, 2)).reshape(own_rows, -1)

    def fold(x):
        return join(jnp.sum(x.reshape(KV, repeat, own_rows, HD), axis=1))

    dealt = dealt.astype(f32)
    grad_query = join(dealt[:, :, :width])
    grad_key = fold(dealt[:, :, width : width + HD])
    grad_value = fold(dealt[:, :, width + HD : width + 2 * HD])
    grad_gain_two = jnp.sum(dealt[:, :, width + 2 * HD : width + 2 * HD + 2], axis=(0, 2))

    def against(w, grad):
        return jnp.sum(w.astype(f32) * grad, axis=1)

    grad_gain_one = against(w_query, grad_query) + against(w_key, grad_key) + against(w_value, grad_value)
    grad_gain_one = grad_gain_one / gain_attn.astype(f32)

    return (
        block_out.reshape(1, piece, depth),
        grad_tokens.reshape(1, piece, depth),
        grad_gain_one,
        grad_query,
        grad_key,
        grad_value,
        grad_out,
        grad_gain_two,
        grad_gate,
        grad_up,
        grad_down,
    )


def solution(mesh):
    rows = P("dp", "seq", None)
    both = P(("dp", "seq"))
    flat = P(("dp", "seq"), None)
    tiles = P("dp", "seq")
    in_specs = (rows, both, flat, flat, flat, flat, both, tiles, tiles, tiles, rows)
    out_specs = (rows, rows, both, flat, flat, flat, flat, both, tiles, tiles, tiles)
    return jax.shard_map(shards, mesh=mesh, in_specs=in_specs, out_specs=out_specs, check_vma=False)
```

```python
import functools

import jax
import jax.numpy as jnp
import numpy as np
from jax import lax
from jax.experimental import pallas as pl
from jax.experimental.pallas import tpu as pltpu
from jax.sharding import PartitionSpec as P

H = 32
KV = 8
HD = 64
LANES = 128
VMEM_BYTES = 50 * 2**20

epsilon = 1e-05
rope_theta = 500000.0
rope_factor = 32.0
old_context = 8192.0

f32 = jnp.float32
bf16 = jnp.bfloat16

NN = (((1,), (0,)), ((), ()))
NT = (((1,), (1,)), ((), ()))
TN = (((0,), (0,)), ((), ()))


def mm(a, b, dims):
    return lax.dot_general(a, b, dims, preferred_element_type=f32)


def cost(flops, moved, transcendentals=0):
    return pl.CostEstimate(flops=flops, bytes_accessed=moved, transcendentals=transcendentals)


def params():
    return pltpu.CompilerParams(vmem_limit_bytes=VMEM_BYTES)


def frequencies(head_size):
    halves = jnp.arange(head_size // 2).astype(f32)
    plain = rope_theta ** (-2.0 * halves / head_size)
    blend = jnp.clip((old_context * plain / (2.0 * jnp.pi) - 1.0) / 3.0, 0.0, 1.0)
    return (1.0 - blend) * plain / rope_factor + blend * plain


def rope_tables(length):
    freq = jnp.tile(frequencies(HD), LANES // (HD // 2))
    angles = jnp.arange(length).astype(f32)[:, None] * freq[None, :]
    sign = jnp.where((jnp.arange(LANES) % HD) < HD // 2, -1.0, 1.0).astype(f32)
    return jnp.cos(angles), jnp.sin(angles) * sign[None, :]


def turn(x, cos, sin):
    lane = lax.broadcasted_iota(jnp.int32, x.shape, 1)
    swapped = jnp.where(
        lane % HD < HD // 2, pltpu.roll(x, LANES - HD // 2, 1), pltpu.roll(x, HD // 2, 1)
    )
    return x * cos + swapped * sin


def qkv_kernel(width, at, mine, other, gain, w, cos, sin, *refs):
    normed, queries, keys_values = refs[-3:]
    x = jnp.where(pl.program_id(0) == 0, mine[...], other[...]).astype(f32)
    inverse = lax.rsqrt(jnp.mean(x * x, axis=-1, keepdims=True) + epsilon)
    low = (x * inverse * gain[...]).astype(bf16)
    normed[...] = low
    y = mm(low, w[:, : width + 2 * HD], NN)
    for first in range(0, width, LANES):
        part = y[:, first : first + LANES]
        queries[:, first : first + LANES] = turn(part, cos[...], sin[...]).astype(bf16)
    part = y[:, width : width + LANES]
    lane = lax.broadcasted_iota(jnp.int32, part.shape, 1)
    keys_values[...] = jnp.where(lane < HD, turn(part, cos[...], sin[...]), part).astype(bf16)


def qkv_call(at, mine, other, gain, w, cos, sin, width, length, held):
    rows, depth = mine.shape
    cols = w.shape[1]

    def whole(shape):
        return pl.BlockSpec(shape, lambda i, at: (0, 0))

    def placed(n):
        return pl.BlockSpec((rows, n), lambda i, at: (at[i], 0))

    return pl.pallas_call(
        functools.partial(qkv_kernel, width),
        grid_spec=pltpu.PrefetchScalarGridSpec(
            num_scalar_prefetch=1,
            grid=(2,),
            in_specs=[
                whole((rows, depth)),
                whole((rows, depth)),
                whole((1, depth)),
                whole((depth, cols)),
                placed(LANES),
                placed(LANES),
            ]
            + [pl.BlockSpec(memory_space=pl.ANY)] * len(held),
            out_specs=[placed(depth), placed(width), placed(2 * HD)],
        ),
        out_shape=[
            jax.ShapeDtypeStruct((length, depth), bf16),
            jax.ShapeDtypeStruct((length, width), bf16),
            jax.ShapeDtypeStruct((length, 2 * HD), bf16),
        ],
        input_output_aliases={7 + i: i for i in range(len(held))},
        compiler_params=params(),
        cost_estimate=cost(4 * rows * depth * cols, 8 * rows * depth + 2 * depth * cols),
        name="qkv",
    )(at, mine, other, gain, w, cos, sin, *held)


def fwd_kernel(bq, share, q_ref, kv_ref, out_ref, ot_ref, lse_ref, m_s, l_s, acc_s):
    i = pl.program_id(0)
    m_s[...] = jnp.full(m_s.shape, -1e30, f32)
    l_s[...] = jnp.zeros(l_s.shape, f32)
    acc_s[...] = jnp.zeros(acc_s.shape, f32)
    qs = q_ref[...] * jnp.asarray(HD**-0.5, bf16)

    def step(j, masked):
        start = pl.multiple_of(j * bq, bq)
        kk = kv_ref[pl.ds(start, bq), :HD]
        vv = kv_ref[pl.ds(start, bq), HD:]
        for h in range(share):
            at = slice(h * HD, (h + 1) * HD)
            s = mm(kk, qs[:, at], NT)
            if masked:
                ki = lax.broadcasted_iota(jnp.int32, s.shape, 0)
                qi = lax.broadcasted_iota(jnp.int32, s.shape, 1)
                s = jnp.where(ki <= qi, s, -1e30)
            m_old = m_s[h : h + 1, :]
            m_new = jnp.maximum(m_old, jnp.max(s, axis=0, keepdims=True))
            p = jnp.exp(s - m_new)
            alpha = jnp.exp(m_old - m_new)
            l_s[h : h + 1, :] = l_s[h : h + 1, :] * alpha + jnp.sum(p, axis=0, keepdims=True)
            m_s[h : h + 1, :] = m_new
            acc_s[at, :] = acc_s[at, :] * alpha + mm(vv, p.astype(bf16), TN)

    def plain(j, carry):
        step(j, False)
        return carry

    lax.fori_loop(0, i, plain, 0)
    step(i, True)
    for h in range(share):
        at = slice(h * HD, (h + 1) * HD)
        total = l_s[h : h + 1, :]
        ot_ref[at, :] = acc_s[at, :] / total
        lse_ref[h : h + 1, :] = m_s[h : h + 1, :] + jnp.log(total)
    out_ref[...] = ot_ref[...].T.astype(bf16)


def attn_fwd(q, kv, bq=1024):
    length, width = q.shape
    share = width // HD
    rows = max(8, share)
    return pl.pallas_call(
        functools.partial(fwd_kernel, bq, share),
        grid=(length // bq,),
        in_specs=[
            pl.BlockSpec((bq, width), lambda i: (i, 0)),
            pl.BlockSpec((length, 2 * HD), lambda i: (0, 0)),
        ],
        out_specs=[
            pl.BlockSpec((bq, width), lambda i: (i, 0)),
            pl.BlockSpec((width, bq), lambda i: (0, i)),
            pl.BlockSpec((rows, bq), lambda i: (0, i)),
        ],
        out_shape=[
            jax.ShapeDtypeStruct((length, width), bf16),
            jax.ShapeDtypeStruct((width, length), f32),
            jax.ShapeDtypeStruct((rows, length), f32),
        ],
        scratch_shapes=[
            pltpu.VMEM((rows, bq), f32),
            pltpu.VMEM((rows, bq), f32),
            pltpu.VMEM((width, bq), f32),
        ],
        compiler_params=params(),
        cost_estimate=cost(8 * length * length * width, 8 * length * width, share * length * length // 2),
        name="attn_fwd",
    )(q, kv)


def bwd_kernel(
    bq, share, q_ref, kv_ref, do_ref, ot_ref, lse_ref, cos_ref, sin_ref, dq_ref, dkv_ref, dqt_s, dk_s, dv_s
):
    i = pl.program_id(0)

    @pl.when(i == 0)
    def _():
        dk_s[...] = jnp.zeros(dk_s.shape, f32)
        dv_s[...] = jnp.zeros(dv_s.shape, f32)

    dqt_s[...] = jnp.zeros(dqt_s.shape, f32)
    qs = q_ref[...] * jnp.asarray(HD**-0.5, bf16)
    do = do_ref[...]
    product = do.astype(f32).T * ot_ref[...]
    inner = [jnp.sum(product[h * HD : (h + 1) * HD], axis=0, keepdims=True) for h in range(share)]

    def step(j, masked):
        start = pl.multiple_of(j * bq, bq)
        kk = kv_ref[pl.ds(start, bq), :HD]
        vv = kv_ref[pl.ds(start, bq), HD:]
        dk = jnp.zeros((bq, HD), f32)
        dv = jnp.zeros((bq, HD), f32)
        for h in range(share):
            at = slice(h * HD, (h + 1) * HD)
            s = mm(kk, qs[:, at], NT)
            p = jnp.exp(s - lse_ref[h : h + 1, :])
            if masked:
                ki = lax.broadcasted_iota(jnp.int32, s.shape, 0)
                qi = lax.broadcasted_iota(jnp.int32, s.shape, 1)
                p = jnp.where(ki <= qi, p, 0.0)
            dp = mm(vv, do[:, at], NT)
            ds = (p * (dp - inner[h])).astype(bf16)
            dv = dv + mm(p.astype(bf16), do[:, at], NN)
            dk = dk + mm(ds, qs[:, at], NN)
            dqt_s[at, :] += mm(kk, ds, TN)
        dk_s[pl.ds(start, bq), :] += dk
        dv_s[pl.ds(start, bq), :] += dv

    def plain(j, carry):
        step(j, False)
        return carry

    lax.fori_loop(0, i, plain, 0)
    step(i, True)
    dq = (dqt_s[...] * (HD**-0.5)).T.astype(bf16).astype(f32)
    rows = pl.ds(pl.multiple_of(i * bq, bq), bq)
    for at in range(0, share * HD, LANES):
        part = dq[:, at : at + LANES]
        dq_ref[:, at : at + LANES] = turn(part, cos_ref[rows, :], -sin_ref[rows, :]).astype(bf16)

    @pl.when(i == pl.num_programs(0) - 1)
    def _():
        both = jnp.concatenate([dk_s[...], dv_s[...]], axis=1).astype(bf16).astype(f32)
        lane = lax.broadcasted_iota(jnp.int32, both.shape, 1)
        turned = turn(both, cos_ref[...], -sin_ref[...])
        dkv_ref[...] = jnp.where(lane < HD, turned, both).astype(bf16)


def attn_bwd(q, kv, do, ot, lse, cos, sin, bq=512):
    length, width = q.shape
    share = width // HD
    rows = lse.shape[0]
    return pl.pallas_call(
        functools.partial(bwd_kernel, bq, share),
        grid=(length // bq,),
        in_specs=[
            pl.BlockSpec((bq, width), lambda i: (i, 0)),
            pl.BlockSpec((length, 2 * HD), lambda i: (0, 0)),
            pl.BlockSpec((bq, width), lambda i: (i, 0)),
            pl.BlockSpec((width, bq), lambda i: (0, i)),
            pl.BlockSpec((rows, bq), lambda i: (0, i)),
            pl.BlockSpec((length, LANES), lambda i: (0, 0)),
            pl.BlockSpec((length, LANES), lambda i: (0, 0)),
        ],
        out_specs=[
            pl.BlockSpec((bq, width), lambda i: (i, 0)),
            pl.BlockSpec((length, 2 * HD), lambda i: (0, 0)),
        ],
        out_shape=[
            jax.ShapeDtypeStruct((length, width), bf16),
            jax.ShapeDtypeStruct((length, 2 * HD), bf16),
        ],
        scratch_shapes=[
            pltpu.VMEM((width, bq), f32),
            pltpu.VMEM((length, HD), f32),
            pltpu.VMEM((length, HD), f32),
        ],
        compiler_params=params(),
        cost_estimate=cost(20 * length * length * width, 16 * length * width, share * length * length // 2),
        name="attn_bwd",
    )(q, kv, do, ot, lse, cos, sin)


def out_kernel(pieces, blocks, at, *refs):
    w_mine, w_other = refs[:pieces], refs[pieces : 2 * pieces]
    mixed, x, gain, middle, normed, acc = refs[2 * pieces :]
    groups = mixed.shape[0]
    depth = x.shape[1]
    half, block, tile = depth // 2, depth // blocks, w_mine[0].shape[1]
    steps = half // tile
    u = pl.program_id(0)
    heads = jnp.concatenate([mixed[at[1 + blocks + g]] for g in range(groups)], axis=1)

    def put(ws, first):
        w = jnp.concatenate([r[...] for r in ws], axis=0)
        acc[:, pl.ds(pl.multiple_of(first, LANES), tile)] = mm(heads, w, NN)

    @pl.when(u < steps)
    def _():
        put(w_mine, at[0] * half + u * tile)

    @pl.when(u >= steps)
    def _():
        put(w_other, (1 - at[0]) * half + (u - steps) * tile)

    @pl.when(u == pl.num_programs(0) - 1)
    def _():
        squares = jnp.zeros((x.shape[0], 1), f32)
        for k in range(blocks):
            here = slice(k * block, (k + 1) * block)
            total = acc[:, pl.ds(pl.multiple_of(at[1 + k] * block, LANES), block)] + x[:, here].astype(f32)
            middle[:, here] = total
            squares = squares + jnp.sum(total * total, axis=-1, keepdims=True)
        inverse = lax.rsqrt(squares / depth + epsilon)
        normed[...] = (middle[...] * inverse * gain[...]).astype(bf16)


def halves_specs(w, tile, steps):
    mine = [pl.BlockSpec((p.shape[0], tile), lambda u, at: (0, jnp.minimum(u, steps - 1))) for p in w]
    other = [pl.BlockSpec((p.shape[0], tile), lambda u, at: (0, jnp.maximum(u - steps, 0))) for p in w]
    return mine + other


def out_call(at, w_mine, w_other, mixed, x, gain, blocks, tile=512):
    groups, rows, part = mixed.shape
    depth = x.shape[1]
    steps = depth // 2 // tile

    def whole(shape):
        return pl.BlockSpec(shape, lambda u, at: (0,) * len(shape))

    return pl.pallas_call(
        functools.partial(out_kernel, len(w_mine), blocks),
        grid_spec=pltpu.PrefetchScalarGridSpec(
            num_scalar_prefetch=1,
            grid=(2 * steps,),
            in_specs=halves_specs(w_mine, tile, steps)
            + [whole(mixed.shape), whole(x.shape), whole((1, depth))],
            out_specs=[whole((rows, depth)), whole((rows, depth))],
            scratch_shapes=[pltpu.VMEM((rows, depth), f32)],
        ),
        out_shape=[
            jax.ShapeDtypeStruct((rows, depth), f32),
            jax.ShapeDtypeStruct((rows, depth), bf16),
        ],
        compiler_params=params(),
        cost_estimate=cost(2 * groups * part * rows * depth, 2 * groups * part * depth + 8 * rows * depth),
        name="out_norm",
    )(at, *w_mine, *w_other, mixed, x, gain)


def ffn_kernel(pieces, *refs):
    x_mine, x_other, c_mine, c_other = refs[:4]
    weights = [refs[4 + i * pieces : 4 + (i + 1) * pieces] for i in range(3)]
    xs, cs, hidden, d_gate, d_up, back_mine, down_mine, back_other, down_other, back, down = refs[-11:]
    u = pl.program_id(0)
    w_gate, w_up, w_down = (jnp.concatenate([r[...] for r in w], axis=0) for w in weights)
    x = jnp.concatenate([x_mine[...], x_other[...]], axis=0)
    c = jnp.concatenate([c_mine[...], c_other[...]], axis=0)
    gate = mm(x, w_gate, NN)
    up = mm(x, w_up, NN)
    grad = mm(c, w_down, NN)
    sig = jax.nn.sigmoid(gate)
    silu = gate * sig
    act = (silu * up).astype(bf16)
    dg = (grad * up * sig * (1.0 + gate * (1.0 - sig))).astype(bf16)
    du = (grad * silu).astype(bf16)
    hidden[...] = act
    d_gate[...] = dg
    d_up[...] = du

    @pl.when(u == 0)
    def _():
        xs[...] = x
        cs[...] = c
        back[...] = mm(dg, w_gate, NT) + mm(du, w_up, NT)
        down[...] = mm(act, w_down, NT)

    @pl.when(u > 0)
    def _():
        back[...] += mm(dg, w_gate, NT) + mm(du, w_up, NT)
        down[...] += mm(act, w_down, NT)

    @pl.when(u == pl.num_programs(0) - 1)
    def _():
        rows = back_mine.shape[0]
        back_mine[...] = back[:rows].astype(bf16)
        down_mine[...] = down[:rows].astype(bf16)
        back_other[...] = back[rows:].astype(bf16)
        down_other[...] = down[rows:].astype(bf16)


def ffn_call(s, count, x_mine, x_other, c_mine, c_other, w_gate, w_up, w_down, held, tile=256):
    rows, depth = x_mine.shape
    units = w_gate[0].shape[1]
    block = pl.BlockSpec((rows, depth), lambda u: (0, 0))
    weights = [pl.BlockSpec((p.shape[0], tile), lambda u: (0, u)) for p in w_gate]
    full = pl.BlockSpec((2 * rows, depth), lambda u: (s, 0))
    act = pl.BlockSpec((2 * rows, tile), lambda u: (s, u))
    full_shape = jax.ShapeDtypeStruct((2 * rows * count, depth), bf16)
    act_shape = jax.ShapeDtypeStruct((2 * rows * count, units), bf16)
    row_shape = jax.ShapeDtypeStruct((rows, depth), bf16)
    first = 4 + 3 * len(w_gate)
    return pl.pallas_call(
        functools.partial(ffn_kernel, len(w_gate)),
        grid=(units // tile,),
        in_specs=[block] * 4 + weights * 3 + [pl.BlockSpec(memory_space=pl.ANY)] * len(held),
        out_specs=[full] * 2 + [act] * 3 + [block] * 4,
        out_shape=[full_shape] * 2 + [act_shape] * 3 + [row_shape] * 4,
        scratch_shapes=[pltpu.VMEM((2 * rows, depth), f32)] * 2,
        input_output_aliases={first + i: i for i in range(len(held))},
        compiler_params=params(),
        cost_estimate=cost(24 * rows * depth * units, 6 * depth * units + 20 * rows * depth + 12 * rows * units),
        name="ffn",
    )(x_mine, x_other, c_mine, c_other, *w_gate, *w_up, *w_down, *held)


def mid_kernel(pieces, blocks, at, *refs):
    w_mine, w_other = refs[:pieces], refs[pieces : 2 * pieces]
    ring, own, swapped, middle, cot, gain, d_middle, branch, d_gain, d_mixed, acc = refs[2 * pieces :]
    rows, depth = middle.shape
    groups, _, part = d_mixed.shape
    half, block, tile = depth // 2, depth // blocks, w_mine[0].shape[1]
    steps = half // tile
    u = pl.program_id(0)

    @pl.when(u == 0)
    def _():
        grad = ring[...].astype(f32) + (own[...].astype(f32) + swapped[...].astype(f32))
        m = middle[...]
        inverse = lax.rsqrt(jnp.mean(m * m, axis=-1, keepdims=True) + epsilon)
        scaled = grad * gain[...]
        slope = jnp.mean(m * scaled, axis=-1, keepdims=True) * (inverse * inverse * inverse)
        total = cot[...].astype(f32) + inverse * scaled - m * slope
        d_middle[...] = total
        for k in range(blocks):
            place = pl.ds(pl.multiple_of(at[1 + k] * block, LANES), block)
            branch[:, place] = total[:, k * block : (k + 1) * block].astype(bf16)
        d_gain[...] = jnp.sum(grad * m * inverse, axis=0, keepdims=True)
        acc[...] = jnp.zeros(acc.shape, f32)

    def add(ws, first):
        w = jnp.concatenate([r[...] for r in ws], axis=0)
        acc[...] += mm(branch[:, pl.ds(pl.multiple_of(first, LANES), tile)], w, NT)

    @pl.when(u < steps)
    def _():
        add(w_mine, at[0] * half + u * tile)

    @pl.when(u >= steps)
    def _():
        add(w_other, (1 - at[0]) * half + (u - steps) * tile)

    @pl.when(u == pl.num_programs(0) - 1)
    def _():
        for g in range(groups):
            d_mixed[at[1 + blocks + g]] = acc[:, g * part : (g + 1) * part].astype(bf16)


def mid_call(at, w_mine, w_other, ring, own, swapped, middle, cot, gain, part, blocks, tile=512):
    rows, depth = middle.shape
    heads = sum(p.shape[0] for p in w_mine)
    groups = heads // part
    steps = depth // 2 // tile

    def whole(shape):
        return pl.BlockSpec(shape, lambda u, at: (0,) * len(shape))

    block, line = whole((rows, depth)), whole((1, depth))
    return pl.pallas_call(
        functools.partial(mid_kernel, len(w_mine), blocks),
        grid_spec=pltpu.PrefetchScalarGridSpec(
            num_scalar_prefetch=1,
            grid=(2 * steps,),
            in_specs=halves_specs(w_mine, tile, steps) + [block] * 5 + [line],
            out_specs=[block, block, line, whole((groups, rows, part))],
            scratch_shapes=[pltpu.VMEM((rows, heads), f32)],
        ),
        out_shape=[
            jax.ShapeDtypeStruct((rows, depth), f32),
            jax.ShapeDtypeStruct((rows, depth), bf16),
            jax.ShapeDtypeStruct((1, depth), f32),
            jax.ShapeDtypeStruct((groups, rows, part), bf16),
        ],
        compiler_params=params(),
        cost_estimate=cost(2 * heads * rows * depth, 2 * heads * depth + 16 * rows * depth),
        name="mid",
    )(at, *w_mine, *w_other, ring, own, swapped, middle, cot, gain)


def first_kernel(blocks, at, ring, own, swapped, x_ref, d_middle, gain, out):
    depth = x_ref.shape[1]
    block = depth // blocks
    grad = ring[...].astype(f32) + (own[...].astype(f32) + swapped[...].astype(f32))
    x = x_ref[...].astype(f32)
    inverse = lax.rsqrt(jnp.mean(x * x, axis=-1, keepdims=True) + epsilon)
    scaled = grad * gain[...]
    slope = jnp.mean(x * scaled, axis=-1, keepdims=True) * (inverse * inverse * inverse)
    total = d_middle[...] + inverse * scaled - x * slope
    for k in range(blocks):
        place = pl.ds(pl.multiple_of(at[1 + k] * block, LANES), block)
        out[:, place] = total[:, k * block : (k + 1) * block].astype(bf16)


def first_call(at, ring, own, swapped, x, d_middle, gain, blocks, tile=64):
    rows, depth = x.shape
    block = pl.BlockSpec((tile, depth), lambda i, at: (i, 0))
    return pl.pallas_call(
        functools.partial(first_kernel, blocks),
        grid_spec=pltpu.PrefetchScalarGridSpec(
            num_scalar_prefetch=1,
            grid=(rows // tile,),
            in_specs=[block] * 5 + [pl.BlockSpec((1, depth), lambda i, at: (0, 0))],
            out_specs=block,
        ),
        out_shape=jax.ShapeDtypeStruct((rows, depth), bf16),
        compiler_params=params(),
        cost_estimate=cost(20 * rows * depth, 14 * rows * depth),
        name="first_norm_back",
    )(at, ring, own, swapped, x, d_middle, gain)


def after(value, *others):
    return lax.optimization_barrier((value,) + others)[0]


def shards(
    tokens, gain_attn, w_query, w_key, w_value, w_out, gain_mlp, w_gate, w_up, w_down, cotangent
):
    groups = lax.axis_size("seq")
    dp_count = lax.axis_size("dp")
    seq_count, piece, depth = tokens.shape
    assert seq_count == 1 and groups >= KV and groups % 2 == 0 and groups % dp_count == 0
    assert dp_count & (dp_count - 1) == 0
    length = piece * groups
    width = H // groups * HD
    repeat = groups // KV
    own_rows = w_query.shape[0]
    half = depth // 2
    block = depth // dp_count

    chips = groups // 2
    middle_chip = chips // 2
    order = list(range(middle_chip)) + list(range(chips - 1, middle_chip - 1, -1))
    place = np.argsort(order)
    follow = [order[(place[c] + 1) % chips] for c in range(chips)]
    ring = [(2 * c + k, 2 * follow[c] + k) for c in range(chips) for k in range(2)]
    swap = [(i, i ^ 1) for i in range(groups)]

    seq_at = lax.axis_index("seq")
    dp_at = lax.axis_index("dp")
    core_at = seq_at % 2
    ring_at = jnp.asarray(place, jnp.int32)[seq_at // 2]
    chunk = jnp.asarray(order, jnp.int32)[(ring_at + chips - jnp.arange(chips)) % chips]
    pair_at = 2 * chunk[:, None] + jnp.stack([core_at, 1 - core_at])[None, :]
    dp_order = dp_at ^ jnp.arange(dp_count)
    group_order = (dp_order[:, None] * (groups // dp_count) + jnp.arange(groups // dp_count)).reshape(-1)
    at = jnp.concatenate([core_at[None], jnp.arange(dp_count), group_order]).astype(jnp.int32)

    def step_ring(x):
        return lax.ppermute(x, "seq", ring)

    def step_swap(x):
        return lax.ppermute(x, "seq", swap)

    def step_dp(x, k):
        return lax.ppermute(x, "dp", [(i, i ^ k) for i in range(dp_count)])

    def rows_at(x, start, count):
        return lax.dynamic_slice_in_dim(x, start, count, 0)

    def cols_at(x, start, count):
        return lax.dynamic_slice_in_dim(x, start, count, 1)

    def gather_dp(x):
        return [x] + [step_dp(x, k) for k in range(1, dp_count)]

    def gather_hops(x):
        if dp_count != 4:
            return gather_dp(x)
        cut = x.shape[0] // 2
        one, two = step_dp(x, 1), step_dp(x, 2)
        return [x, one, two, step_dp(one[:cut], 2), step_dp(two[cut:], 1)]

    def scatter_dp(parts):
        return [step_dp(parts[k], k) for k in range(1, dp_count)]

    def full_weight(w):
        return [lax.all_gather(w, "dp", axis=0, tiled=True)]

    def owned_grad(grad):
        return lax.psum_scatter(grad, "dp", scatter_dimension=0, tiled=True)

    def pair_sides(own, got):
        return jnp.where(core_at == 0, jnp.concatenate([own, got]), jnp.concatenate([got, own]))

    x_own = tokens.reshape(piece, depth)
    cot_own = cotangent.reshape(piece, depth)

    def per_group(w):
        return jnp.repeat(w.reshape(own_rows, KV, HD), repeat, axis=1)

    with jax.named_scope("projection_columns"):
        gains_own = jnp.stack([gain_attn, gain_mlp], axis=-1)
        gains_own = jnp.pad(gains_own, ((0, 0), (0, LANES - 2)))
        gains_own = jnp.broadcast_to(gains_own[:, None, :], (own_rows, groups, LANES))
        own_cols = jnp.concatenate(
            [w_query.reshape(own_rows, groups, width), per_group(w_key), per_group(w_value), gains_own],
            axis=-1,
        )
        cols = own_cols.shape[-1]
        dp_rows = groups * own_rows
        cols_dp = lax.all_to_all(jnp.transpose(own_cols, (1, 0, 2)), "seq", 0, 0, tiled=True)
        cols_dp = cols_dp.reshape(dp_rows, cols)

    with jax.named_scope("tokens_ring"):
        x_mine = [x_own, step_ring(after(x_own, own_cols))]

    with jax.named_scope("projection_columns"):
        cols_all = jnp.zeros((depth, cols), bf16)
        for k, part in enumerate(gather_dp(cols_dp)):
            cols_all = lax.dynamic_update_slice_in_dim(cols_all, part, dp_order[k] * dp_rows, 0)
        w_qkv = cols_all[:, : width + 2 * HD]
        gains = jnp.transpose(cols_all[:, width + 2 * HD : width + 2 * HD + 2].astype(f32))
        gain_one, gain_two = gains[:1], gains[1:]

    with jax.named_scope("tokens_ring"):
        for s in range(2, chips):
            x_mine.append(step_ring(after(x_mine[-1], cols_dp if s == 2 else cols_all)))
        x_other = [step_swap(x) for x in x_mine]

    with jax.named_scope("out_weight"):
        keep = cols_at(w_out, core_at * half, half)
        give = cols_at(w_out, (1 - core_at) * half, half)
        chip_rows = [pair_sides(keep, step_swap(give))]
        for s in range(1, chips):
            chip_rows.append(step_ring(after(chip_rows[0], x_mine[-1]) if s == 1 else chip_rows[-1]))
        out_rows = jnp.zeros((dp_rows, half), bf16)
        for s in range(chips):
            out_rows = lax.dynamic_update_slice_in_dim(out_rows, chip_rows[s], chunk[s] * 2 * own_rows, 0)

        out_mine = gather_hops(out_rows)
        out_other = [step_swap(p) for p in out_mine]

    with jax.named_scope("feed_forward_weights"):
        gate_full, up_full, down_full = full_weight(w_gate), full_weight(w_up), full_weight(w_down)

    cos, sin = rope_tables(length)

    held = ()
    for s in range(chips):
        held = qkv_call(
            pair_at[s], x_mine[s], after(x_other[s], chip_rows[s]), gain_one, cols_all, cos, sin, width, length, held
        )
    normed, queries, keys_values = held

    with jax.named_scope("cotangent_ring"):
        c_mine = [cot_own, step_ring(after(cot_own, chip_rows[-1]))]
        c_other = [step_swap(c) for c in c_mine]

    head_out, out_t, lse = attn_fwd(queries, keys_values)
    with jax.named_scope("mixed"):
        head_out = after(head_out, c_mine[1]).reshape(groups, piece, width)
        mixed = lax.all_to_all(head_out, "seq", 0, 0, tiled=True)
    middle, normed_two = out_call(at, out_mine, out_other, mixed, x_own, gain_two, dp_count)

    def add(*parts):
        total = parts[0].astype(f32)
        for p in parts[1:]:
            total = total + p.astype(f32)
        return total

    def weight_grad(rows, grads):
        return mm(rows, grads, TN).astype(bf16)

    n_mine = [normed_two]
    for s in range(1, chips):
        if s + 1 < chips:
            with jax.named_scope("cotangent_ring"):
                c_mine.append(step_ring(after(c_mine[-1], mixed if s == 1 else n_mine[-1])))
                c_other.append(step_swap(c_mine[-1]))
        with jax.named_scope("normed_ring"):
            n_mine.append(step_ring(n_mine[-1] if s == 1 else after(n_mine[-1], c_mine[-1])))
    with jax.named_scope("normed_ring"):
        n_other = [step_swap(n) for n in n_mine]

    ffn, held, acc = [], (), None
    for s in range(chips):
        n_here = n_other[s] if acc is None else after(n_other[s], acc)
        out = ffn_call(
            s, chips, n_mine[s], n_here, c_mine[s], c_other[s], gate_full, up_full, down_full, held
        )
        held, rest = out[:5], out[5:]
        with jax.named_scope("feed_forward_pair"):
            back_swapped = step_swap(rest[2])
            down_swapped = step_swap(rest[3])
        ffn.append((rest[0], rest[1], back_swapped, down_swapped))
        if s:
            with jax.named_scope("back_ring"):
                so_far = add(ffn[s][0]) if acc is None else add(step_ring(acc), ffn[s][0])
                acc = add(lax.optimization_barrier(so_far), ffn[s][2]).astype(bf16)
    n_all, c_all, hidden, d_gate, d_up = held
    n_all = after(n_all, acc)
    with jax.named_scope("back_ring"):
        back_got = step_ring(acc)

    with jax.named_scope("gate_grad"):
        gate_part = weight_grad(n_all, d_gate)
        grad_gate = owned_grad(gate_part)
    with jax.named_scope("up_grad"):
        up_part = weight_grad(n_all, d_up)
        grad_up = owned_grad(up_part)
    back_got = after(back_got, gate_part, up_part)

    d_middle, branch, d_gain_two, d_mixed = mid_call(
        at, out_mine, out_other, back_got, ffn[0][0], ffn[0][2], middle, cot_own, gain_two, width, dp_count
    )
    with jax.named_scope("d_mixed"):
        d_heads = lax.all_to_all(d_mixed, "seq", 0, 0, tiled=True).reshape(length, width)

    with jax.named_scope("out_grad"):

        def out_part(start):
            g = jnp.einsum("gnh,nd->ghd", mixed, cols_at(branch, start, half), preferred_element_type=f32)
            return g.reshape(groups * width, half).astype(bf16)

        out_theirs = out_part((1 - core_at) * half)
        out_theirs_sent = step_swap(out_theirs)
        out_own = out_part(core_at * half)
    with jax.named_scope("down_grad"):
        down_rows, _ = lax.optimization_barrier((c_all, branch))
        down_part = weight_grad(down_rows, hidden)
        grad_down = owned_grad(down_part)

    with jax.named_scope("down_ring"):
        acc = add(after(ffn[1][1], back_got), ffn[1][3]).astype(bf16)
        down_two = step_ring(acc)

    with jax.named_scope("out_grad"):
        out_sum = add(out_own, out_theirs_sent).astype(bf16)
        out_dp = owned_grad(out_sum)

    d_heads = after(d_heads, down_part, out_sum)

    d_queries, d_kv = attn_bwd(queries, keys_values, d_heads, out_t, lse, cos, sin)

    with jax.named_scope("down_ring"):
        for s in range(2, chips):
            acc = add(after(down_two, d_heads if s == 2 else d_kv), ffn[s][1], ffn[s][3]).astype(bf16)
            down_two = step_ring(acc)

    with jax.named_scope("first_ring"):
        def d_normed(s, side):
            d_q = rows_at(d_queries, pair_at[s, side] * piece, piece)
            d_k = rows_at(d_kv, pair_at[s, side] * piece, piece)
            return mm(jnp.concatenate([d_q, d_k], axis=1), w_qkv, NT).astype(bf16)

        steps = list(range(1, chips)) + [0]
        theirs = {s: step_swap(d_normed(s, 1)) for s in steps}
        own = {s: d_normed(s, 0) for s in steps}
        first_acc = [add(own[1], theirs[1]).astype(bf16)]
        for s in range(2, chips):
            first_acc.append(add(step_ring(first_acc[-1]), own[s], theirs[s]).astype(bf16))
        first_got = step_ring(first_acc[-1])

    with jax.named_scope("projection_grads"):
        d_qkv = jnp.concatenate([d_queries, d_kv], axis=1)
        grad_cols = mm(after(normed, first_acc[0]), d_qkv, TN).astype(bf16)
        high = d_gain_two.astype(bf16)
        rest = (d_gain_two - high.astype(f32)).astype(bf16)
        extra = jnp.pad(jnp.transpose(jnp.concatenate([high, rest], axis=0)), ((0, 0), (0, LANES - 2)))
        grad_cols = jnp.concatenate([grad_cols, extra], axis=1)
        col_parts = [rows_at(grad_cols, dp_order[k] * block, block) for k in range(dp_count)]
        col_sent = [after(p, first_acc[1]) for p in scatter_dp(col_parts)]
        total = add(col_parts[0], *col_sent).astype(bf16)
        dealt = lax.all_to_all(total.reshape(groups, own_rows, cols), "seq", 0, 0, tiled=True)

    with jax.named_scope("feed_forward_grads"):
        grads = lax.optimization_barrier((grad_gate, grad_up, grad_down, first_acc[-1]))
        grad_gate, grad_up, grad_down = (g.astype(f32) for g in grads[:3])

    with jax.named_scope("out_grad"):
        same_core = [[2 * c + k for c in range(chips)] for k in range(2)]
        out_dp = after(out_dp, first_acc[-1]).reshape(chips, 2 * own_rows, half)
        out_terms = lax.all_to_all(out_dp, "seq", 0, 0, axis_index_groups=same_core, tiled=True)
        acc = jnp.sum(out_terms.astype(f32), axis=0)
        out_keep = rows_at(acc, core_at * own_rows, own_rows)
        out_give = rows_at(acc, (1 - core_at) * own_rows, own_rows).astype(bf16)
        out_take = step_swap(out_give).astype(f32)
        grad_out = jnp.where(
            core_at == 0,
            jnp.concatenate([out_keep, out_take], axis=1),
            jnp.concatenate([out_take, out_keep], axis=1),
        )

    grad_tokens = first_call(at, first_got, own[0], theirs[0], x_own, d_middle, gain_one, dp_count)
    block_out = (middle + add(down_two, ffn[0][1], ffn[0][3])).astype(bf16)

    def join(x):
        return jnp.transpose(x, (1, 0, 2)).reshape(own_rows, -1)

    def fold(x):
        return join(jnp.sum(x.reshape(KV, repeat, own_rows, HD), axis=1))

    dealt = after(dealt, first_acc[-1]).astype(f32)
    grad_query = join(dealt[:, :, :width])
    grad_key = fold(dealt[:, :, width : width + HD])
    grad_value = fold(dealt[:, :, width + HD : width + 2 * HD])
    grad_gain_two = jnp.sum(dealt[:, :, width + 2 * HD : width + 2 * HD + 2], axis=(0, 2))

    def against(w, grad):
        return jnp.sum(w.astype(f32) * grad, axis=1)

    grad_gain_one = against(w_query, grad_query) + against(w_key, grad_key) + against(w_value, grad_value)
    grad_gain_one = grad_gain_one / gain_attn.astype(f32)

    return (
        block_out.reshape(1, piece, depth),
        grad_tokens.reshape(1, piece, depth),
        grad_gain_one,
        grad_query,
        grad_key,
        grad_value,
        grad_out,
        grad_gain_two,
        grad_gate,
        grad_up,
        grad_down,
    )


def solution(mesh):
    rows = P("dp", "seq", None)
    both = P(("dp", "seq"))
    flat = P(("dp", "seq"), None)
    tiles = P("dp", "seq")
    in_specs = (rows, both, flat, flat, flat, flat, both, tiles, tiles, tiles, rows)
    out_specs = (rows, rows, both, flat, flat, flat, flat, both, tiles, tiles, tiles)
    return jax.shard_map(shards, mesh=mesh, in_specs=in_specs, out_specs=out_specs, check_vma=False)
```

```python
import functools

import jax
import jax.numpy as jnp
import numpy as np
from jax import lax
from jax.experimental import pallas as pl
from jax.experimental.pallas import tpu as pltpu
from jax.sharding import PartitionSpec as P

H = 32
KV = 8
HD = 64
LANES = 128
VMEM_BYTES = 50 * 2**20

epsilon = 1e-05
rope_theta = 500000.0
rope_factor = 32.0
old_context = 8192.0

f32 = jnp.float32
bf16 = jnp.bfloat16

NN = (((1,), (0,)), ((), ()))
NT = (((1,), (1,)), ((), ()))
TN = (((0,), (0,)), ((), ()))


def mm(a, b, dims):
    return lax.dot_general(a, b, dims, preferred_element_type=f32)


def cost(flops, moved, transcendentals=0):
    return pl.CostEstimate(flops=flops, bytes_accessed=moved, transcendentals=transcendentals)


def params():
    return pltpu.CompilerParams(vmem_limit_bytes=VMEM_BYTES)


def frequencies(head_size):
    halves = jnp.arange(head_size // 2).astype(f32)
    plain = rope_theta ** (-2.0 * halves / head_size)
    blend = jnp.clip((old_context * plain / (2.0 * jnp.pi) - 1.0) / 3.0, 0.0, 1.0)
    return (1.0 - blend) * plain / rope_factor + blend * plain


def rope_tables(length):
    freq = jnp.tile(frequencies(HD), LANES // (HD // 2))
    angles = jnp.arange(length).astype(f32)[:, None] * freq[None, :]
    sign = jnp.where((jnp.arange(LANES) % HD) < HD // 2, -1.0, 1.0).astype(f32)
    return jnp.cos(angles), jnp.sin(angles) * sign[None, :]


def turn(x, cos, sin):
    lane = lax.broadcasted_iota(jnp.int32, x.shape, 1)
    swapped = jnp.where(
        lane % HD < HD // 2, pltpu.roll(x, LANES - HD // 2, 1), pltpu.roll(x, HD // 2, 1)
    )
    return x * cos + swapped * sin


def qkv_kernel(width, at, mine, other, gain, w, cos, sin, *refs):
    normed, queries, keys_values = refs[-3:]
    x = jnp.where(pl.program_id(0) == 0, mine[...], other[...]).astype(f32)
    inverse = lax.rsqrt(jnp.mean(x * x, axis=-1, keepdims=True) + epsilon)
    low = (x * inverse * gain[...]).astype(bf16)
    normed[...] = low
    y = mm(low, w[:, : width + 2 * HD], NN)
    for first in range(0, width, LANES):
        part = y[:, first : first + LANES]
        queries[:, first : first + LANES] = turn(part, cos[...], sin[...]).astype(bf16)
    part = y[:, width : width + LANES]
    lane = lax.broadcasted_iota(jnp.int32, part.shape, 1)
    keys_values[...] = jnp.where(lane < HD, turn(part, cos[...], sin[...]), part).astype(bf16)


def qkv_call(at, mine, other, gain, w, cos, sin, width, length, held):
    rows, depth = mine.shape
    cols = w.shape[1]

    def whole(shape):
        return pl.BlockSpec(shape, lambda i, at: (0, 0))

    def placed(n):
        return pl.BlockSpec((rows, n), lambda i, at: (at[i], 0))

    return pl.pallas_call(
        functools.partial(qkv_kernel, width),
        grid_spec=pltpu.PrefetchScalarGridSpec(
            num_scalar_prefetch=1,
            grid=(2,),
            in_specs=[
                whole((rows, depth)),
                whole((rows, depth)),
                whole((1, depth)),
                whole((depth, cols)),
                placed(LANES),
                placed(LANES),
            ]
            + [pl.BlockSpec(memory_space=pl.ANY)] * len(held),
            out_specs=[placed(depth), placed(width), placed(2 * HD)],
        ),
        out_shape=[
            jax.ShapeDtypeStruct((length, depth), bf16),
            jax.ShapeDtypeStruct((length, width), bf16),
            jax.ShapeDtypeStruct((length, 2 * HD), bf16),
        ],
        input_output_aliases={7 + i: i for i in range(len(held))},
        compiler_params=params(),
        cost_estimate=cost(4 * rows * depth * cols, 8 * rows * depth + 2 * depth * cols),
        name="qkv",
    )(at, mine, other, gain, w, cos, sin, *held)


def fwd_kernel(bq, share, q_ref, kv_ref, out_ref, ot_ref, lse_ref, m_s, l_s, acc_s):
    i = pl.program_id(0)
    m_s[...] = jnp.full(m_s.shape, -1e30, f32)
    l_s[...] = jnp.zeros(l_s.shape, f32)
    acc_s[...] = jnp.zeros(acc_s.shape, f32)
    qs = q_ref[...] * jnp.asarray(HD**-0.5, bf16)

    def step(j, masked):
        start = pl.multiple_of(j * bq, bq)
        kk = kv_ref[pl.ds(start, bq), :HD]
        vv = kv_ref[pl.ds(start, bq), HD:]
        for h in range(share):
            at = slice(h * HD, (h + 1) * HD)
            s = mm(kk, qs[:, at], NT)
            if masked:
                ki = lax.broadcasted_iota(jnp.int32, s.shape, 0)
                qi = lax.broadcasted_iota(jnp.int32, s.shape, 1)
                s = jnp.where(ki <= qi, s, -1e30)
            m_old = m_s[h : h + 1, :]
            m_new = jnp.maximum(m_old, jnp.max(s, axis=0, keepdims=True))
            p = jnp.exp(s - m_new)
            alpha = jnp.exp(m_old - m_new)
            l_s[h : h + 1, :] = l_s[h : h + 1, :] * alpha + jnp.sum(p, axis=0, keepdims=True)
            m_s[h : h + 1, :] = m_new
            acc_s[at, :] = acc_s[at, :] * alpha + mm(vv, p.astype(bf16), TN)

    def plain(j, carry):
        step(j, False)
        return carry

    lax.fori_loop(0, i, plain, 0)
    step(i, True)
    for h in range(share):
        at = slice(h * HD, (h + 1) * HD)
        total = l_s[h : h + 1, :]
        ot_ref[at, :] = acc_s[at, :] / total
        lse_ref[h : h + 1, :] = m_s[h : h + 1, :] + jnp.log(total)
    out_ref[...] = ot_ref[...].T.astype(bf16)


def attn_fwd(q, kv, bq=1024):
    length, width = q.shape
    share = width // HD
    rows = max(8, share)
    return pl.pallas_call(
        functools.partial(fwd_kernel, bq, share),
        grid=(length // bq,),
        in_specs=[
            pl.BlockSpec((bq, width), lambda i: (i, 0)),
            pl.BlockSpec((length, 2 * HD), lambda i: (0, 0)),
        ],
        out_specs=[
            pl.BlockSpec((bq, width), lambda i: (i, 0)),
            pl.BlockSpec((width, bq), lambda i: (0, i)),
            pl.BlockSpec((rows, bq), lambda i: (0, i)),
        ],
        out_shape=[
            jax.ShapeDtypeStruct((length, width), bf16),
            jax.ShapeDtypeStruct((width, length), f32),
            jax.ShapeDtypeStruct((rows, length), f32),
        ],
        scratch_shapes=[
            pltpu.VMEM((rows, bq), f32),
            pltpu.VMEM((rows, bq), f32),
            pltpu.VMEM((width, bq), f32),
        ],
        compiler_params=params(),
        cost_estimate=cost(8 * length * length * width, 8 * length * width, share * length * length // 2),
        name="attn_fwd",
    )(q, kv)


def bwd_kernel(
    bq, share, q_ref, kv_ref, do_ref, ot_ref, lse_ref, cos_ref, sin_ref, dq_ref, dkv_ref, dqt_s, dk_s, dv_s
):
    i = pl.program_id(0)

    @pl.when(i == 0)
    def _():
        dk_s[...] = jnp.zeros(dk_s.shape, f32)
        dv_s[...] = jnp.zeros(dv_s.shape, f32)

    dqt_s[...] = jnp.zeros(dqt_s.shape, f32)
    qs = q_ref[...] * jnp.asarray(HD**-0.5, bf16)
    do = do_ref[...]
    product = do.astype(f32).T * ot_ref[...]
    inner = [jnp.sum(product[h * HD : (h + 1) * HD], axis=0, keepdims=True) for h in range(share)]

    def step(j, masked):
        start = pl.multiple_of(j * bq, bq)
        kk = kv_ref[pl.ds(start, bq), :HD]
        vv = kv_ref[pl.ds(start, bq), HD:]
        dk = jnp.zeros((bq, HD), f32)
        dv = jnp.zeros((bq, HD), f32)
        for h in range(share):
            at = slice(h * HD, (h + 1) * HD)
            s = mm(kk, qs[:, at], NT)
            p = jnp.exp(s - lse_ref[h : h + 1, :])
            if masked:
                ki = lax.broadcasted_iota(jnp.int32, s.shape, 0)
                qi = lax.broadcasted_iota(jnp.int32, s.shape, 1)
                p = jnp.where(ki <= qi, p, 0.0)
            dp = mm(vv, do[:, at], NT)
            ds = (p * (dp - inner[h])).astype(bf16)
            dv = dv + mm(p.astype(bf16), do[:, at], NN)
            dk = dk + mm(ds, qs[:, at], NN)
            dqt_s[at, :] += mm(kk, ds, TN)
        dk_s[pl.ds(start, bq), :] += dk
        dv_s[pl.ds(start, bq), :] += dv

    def plain(j, carry):
        step(j, False)
        return carry

    lax.fori_loop(0, i, plain, 0)
    step(i, True)
    dq = (dqt_s[...] * (HD**-0.5)).T.astype(bf16).astype(f32)
    rows = pl.ds(pl.multiple_of(i * bq, bq), bq)
    for at in range(0, share * HD, LANES):
        part = dq[:, at : at + LANES]
        dq_ref[:, at : at + LANES] = turn(part, cos_ref[rows, :], -sin_ref[rows, :]).astype(bf16)

    @pl.when(i == pl.num_programs(0) - 1)
    def _():
        both = jnp.concatenate([dk_s[...], dv_s[...]], axis=1).astype(bf16).astype(f32)
        lane = lax.broadcasted_iota(jnp.int32, both.shape, 1)
        turned = turn(both, cos_ref[...], -sin_ref[...])
        dkv_ref[...] = jnp.where(lane < HD, turned, both).astype(bf16)


def attn_bwd(q, kv, do, ot, lse, cos, sin, bq=512):
    length, width = q.shape
    share = width // HD
    rows = lse.shape[0]
    return pl.pallas_call(
        functools.partial(bwd_kernel, bq, share),
        grid=(length // bq,),
        in_specs=[
            pl.BlockSpec((bq, width), lambda i: (i, 0)),
            pl.BlockSpec((length, 2 * HD), lambda i: (0, 0)),
            pl.BlockSpec((bq, width), lambda i: (i, 0)),
            pl.BlockSpec((width, bq), lambda i: (0, i)),
            pl.BlockSpec((rows, bq), lambda i: (0, i)),
            pl.BlockSpec((length, LANES), lambda i: (0, 0)),
            pl.BlockSpec((length, LANES), lambda i: (0, 0)),
        ],
        out_specs=[
            pl.BlockSpec((bq, width), lambda i: (i, 0)),
            pl.BlockSpec((length, 2 * HD), lambda i: (0, 0)),
        ],
        out_shape=[
            jax.ShapeDtypeStruct((length, width), bf16),
            jax.ShapeDtypeStruct((length, 2 * HD), bf16),
        ],
        scratch_shapes=[
            pltpu.VMEM((width, bq), f32),
            pltpu.VMEM((length, HD), f32),
            pltpu.VMEM((length, HD), f32),
        ],
        compiler_params=params(),
        cost_estimate=cost(20 * length * length * width, 16 * length * width, share * length * length // 2),
        name="attn_bwd",
    )(q, kv, do, ot, lse, cos, sin)


def out_kernel(pieces, blocks, at, *refs):
    w_mine, w_other = refs[:pieces], refs[pieces : 2 * pieces]
    mixed, x, gain, middle, normed, acc = refs[2 * pieces :]
    groups = mixed.shape[0]
    depth = x.shape[1]
    half, block, tile = depth // 2, depth // blocks, w_mine[0].shape[1]
    steps = half // tile
    u = pl.program_id(0)
    heads = jnp.concatenate([mixed[at[1 + blocks + g]] for g in range(groups)], axis=1)

    def put(ws, first):
        w = jnp.concatenate([r[...] for r in ws], axis=0)
        acc[:, pl.ds(pl.multiple_of(first, LANES), tile)] = mm(heads, w, NN)

    @pl.when(u < steps)
    def _():
        put(w_mine, at[0] * half + u * tile)

    @pl.when(u >= steps)
    def _():
        put(w_other, (1 - at[0]) * half + (u - steps) * tile)

    @pl.when(u == pl.num_programs(0) - 1)
    def _():
        squares = jnp.zeros((x.shape[0], 1), f32)
        for k in range(blocks):
            here = slice(k * block, (k + 1) * block)
            total = acc[:, pl.ds(pl.multiple_of(at[1 + k] * block, LANES), block)] + x[:, here].astype(f32)
            middle[:, here] = total
            squares = squares + jnp.sum(total * total, axis=-1, keepdims=True)
        inverse = lax.rsqrt(squares / depth + epsilon)
        normed[...] = (middle[...] * inverse * gain[...]).astype(bf16)


def halves_specs(w, tile, steps):
    mine = [pl.BlockSpec((p.shape[0], tile), lambda u, at: (0, jnp.minimum(u, steps - 1))) for p in w]
    other = [pl.BlockSpec((p.shape[0], tile), lambda u, at: (0, jnp.maximum(u - steps, 0))) for p in w]
    return mine + other


def out_call(at, w_mine, w_other, mixed, x, gain, blocks, tile=512):
    groups, rows, part = mixed.shape
    depth = x.shape[1]
    steps = depth // 2 // tile

    def whole(shape):
        return pl.BlockSpec(shape, lambda u, at: (0,) * len(shape))

    return pl.pallas_call(
        functools.partial(out_kernel, len(w_mine), blocks),
        grid_spec=pltpu.PrefetchScalarGridSpec(
            num_scalar_prefetch=1,
            grid=(2 * steps,),
            in_specs=halves_specs(w_mine, tile, steps)
            + [whole(mixed.shape), whole(x.shape), whole((1, depth))],
            out_specs=[whole((rows, depth)), whole((rows, depth))],
            scratch_shapes=[pltpu.VMEM((rows, depth), f32)],
        ),
        out_shape=[
            jax.ShapeDtypeStruct((rows, depth), f32),
            jax.ShapeDtypeStruct((rows, depth), bf16),
        ],
        compiler_params=params(),
        cost_estimate=cost(2 * groups * part * rows * depth, 2 * groups * part * depth + 8 * rows * depth),
        name="out_norm",
    )(at, *w_mine, *w_other, mixed, x, gain)


def ffn_kernel(pieces, *refs):
    x_mine, x_other, c_mine, c_other = refs[:4]
    weights = [refs[4 + i * pieces : 4 + (i + 1) * pieces] for i in range(3)]
    xs, cs, hidden, d_gate, d_up, back_mine, down_mine, back_other, down_other, back, down = refs[-11:]
    u = pl.program_id(0)
    w_gate, w_up, w_down = (jnp.concatenate([r[...] for r in w], axis=0) for w in weights)
    x = jnp.concatenate([x_mine[...], x_other[...]], axis=0)
    c = jnp.concatenate([c_mine[...], c_other[...]], axis=0)
    gate = mm(x, w_gate, NN)
    up = mm(x, w_up, NN)
    grad = mm(c, w_down, NN)
    sig = jax.nn.sigmoid(gate)
    silu = gate * sig
    act = (silu * up).astype(bf16)
    dg = (grad * up * sig * (1.0 + gate * (1.0 - sig))).astype(bf16)
    du = (grad * silu).astype(bf16)
    hidden[...] = act
    d_gate[...] = dg
    d_up[...] = du

    @pl.when(u == 0)
    def _():
        xs[...] = x
        cs[...] = c
        back[...] = mm(dg, w_gate, NT) + mm(du, w_up, NT)
        down[...] = mm(act, w_down, NT)

    @pl.when(u > 0)
    def _():
        back[...] += mm(dg, w_gate, NT) + mm(du, w_up, NT)
        down[...] += mm(act, w_down, NT)

    @pl.when(u == pl.num_programs(0) - 1)
    def _():
        rows = back_mine.shape[0]
        back_mine[...] = back[:rows].astype(bf16)
        down_mine[...] = down[:rows].astype(bf16)
        back_other[...] = back[rows:].astype(bf16)
        down_other[...] = down[rows:].astype(bf16)


def ffn_call(s, count, x_mine, x_other, c_mine, c_other, w_gate, w_up, w_down, held, tile=256):
    rows, depth = x_mine.shape
    units = w_gate[0].shape[1]
    block = pl.BlockSpec((rows, depth), lambda u: (0, 0))
    weights = [pl.BlockSpec((p.shape[0], tile), lambda u: (0, u)) for p in w_gate]
    full = pl.BlockSpec((2 * rows, depth), lambda u: (s, 0))
    act = pl.BlockSpec((2 * rows, tile), lambda u: (s, u))
    full_shape = jax.ShapeDtypeStruct((2 * rows * count, depth), bf16)
    act_shape = jax.ShapeDtypeStruct((2 * rows * count, units), bf16)
    row_shape = jax.ShapeDtypeStruct((rows, depth), bf16)
    first = 4 + 3 * len(w_gate)
    return pl.pallas_call(
        functools.partial(ffn_kernel, len(w_gate)),
        grid=(units // tile,),
        in_specs=[block] * 4 + weights * 3 + [pl.BlockSpec(memory_space=pl.ANY)] * len(held),
        out_specs=[full] * 2 + [act] * 3 + [block] * 4,
        out_shape=[full_shape] * 2 + [act_shape] * 3 + [row_shape] * 4,
        scratch_shapes=[pltpu.VMEM((2 * rows, depth), f32)] * 2,
        input_output_aliases={first + i: i for i in range(len(held))},
        compiler_params=params(),
        cost_estimate=cost(24 * rows * depth * units, 6 * depth * units + 20 * rows * depth + 12 * rows * units),
        name="ffn",
    )(x_mine, x_other, c_mine, c_other, *w_gate, *w_up, *w_down, *held)


def mid_kernel(pieces, blocks, at, *refs):
    w_mine, w_other = refs[:pieces], refs[pieces : 2 * pieces]
    ring, own, swapped, middle, cot, gain, d_middle, branch, d_gain, d_mixed, acc = refs[2 * pieces :]
    rows, depth = middle.shape
    groups, _, part = d_mixed.shape
    half, block, tile = depth // 2, depth // blocks, w_mine[0].shape[1]
    steps = half // tile
    u = pl.program_id(0)

    @pl.when(u == 0)
    def _():
        grad = ring[...].astype(f32) + (own[...].astype(f32) + swapped[...].astype(f32))
        m = middle[...]
        inverse = lax.rsqrt(jnp.mean(m * m, axis=-1, keepdims=True) + epsilon)
        scaled = grad * gain[...]
        slope = jnp.mean(m * scaled, axis=-1, keepdims=True) * (inverse * inverse * inverse)
        total = cot[...].astype(f32) + inverse * scaled - m * slope
        d_middle[...] = total
        for k in range(blocks):
            place = pl.ds(pl.multiple_of(at[1 + k] * block, LANES), block)
            branch[:, place] = total[:, k * block : (k + 1) * block].astype(bf16)
        d_gain[...] = jnp.sum(grad * m * inverse, axis=0, keepdims=True)
        acc[...] = jnp.zeros(acc.shape, f32)

    def add(ws, first):
        w = jnp.concatenate([r[...] for r in ws], axis=0)
        acc[...] += mm(branch[:, pl.ds(pl.multiple_of(first, LANES), tile)], w, NT)

    @pl.when(u < steps)
    def _():
        add(w_mine, at[0] * half + u * tile)

    @pl.when(u >= steps)
    def _():
        add(w_other, (1 - at[0]) * half + (u - steps) * tile)

    @pl.when(u == pl.num_programs(0) - 1)
    def _():
        for g in range(groups):
            d_mixed[at[1 + blocks + g]] = acc[:, g * part : (g + 1) * part].astype(bf16)


def mid_call(at, w_mine, w_other, ring, own, swapped, middle, cot, gain, part, blocks, tile=512):
    rows, depth = middle.shape
    heads = sum(p.shape[0] for p in w_mine)
    groups = heads // part
    steps = depth // 2 // tile

    def whole(shape):
        return pl.BlockSpec(shape, lambda u, at: (0,) * len(shape))

    block, line = whole((rows, depth)), whole((1, depth))
    return pl.pallas_call(
        functools.partial(mid_kernel, len(w_mine), blocks),
        grid_spec=pltpu.PrefetchScalarGridSpec(
            num_scalar_prefetch=1,
            grid=(2 * steps,),
            in_specs=halves_specs(w_mine, tile, steps) + [block] * 5 + [line],
            out_specs=[block, block, line, whole((groups, rows, part))],
            scratch_shapes=[pltpu.VMEM((rows, heads), f32)],
        ),
        out_shape=[
            jax.ShapeDtypeStruct((rows, depth), f32),
            jax.ShapeDtypeStruct((rows, depth), bf16),
            jax.ShapeDtypeStruct((1, depth), f32),
            jax.ShapeDtypeStruct((groups, rows, part), bf16),
        ],
        compiler_params=params(),
        cost_estimate=cost(2 * heads * rows * depth, 2 * heads * depth + 16 * rows * depth),
        name="mid",
    )(at, *w_mine, *w_other, ring, own, swapped, middle, cot, gain)


def first_kernel(blocks, at, ring, own, swapped, x_ref, d_middle, gain, out):
    depth = x_ref.shape[1]
    block = depth // blocks
    grad = ring[...].astype(f32) + (own[...].astype(f32) + swapped[...].astype(f32))
    x = x_ref[...].astype(f32)
    inverse = lax.rsqrt(jnp.mean(x * x, axis=-1, keepdims=True) + epsilon)
    scaled = grad * gain[...]
    slope = jnp.mean(x * scaled, axis=-1, keepdims=True) * (inverse * inverse * inverse)
    total = d_middle[...] + inverse * scaled - x * slope
    for k in range(blocks):
        place = pl.ds(pl.multiple_of(at[1 + k] * block, LANES), block)
        out[:, place] = total[:, k * block : (k + 1) * block].astype(bf16)


def first_call(at, ring, own, swapped, x, d_middle, gain, blocks, tile=64):
    rows, depth = x.shape
    block = pl.BlockSpec((tile, depth), lambda i, at: (i, 0))
    return pl.pallas_call(
        functools.partial(first_kernel, blocks),
        grid_spec=pltpu.PrefetchScalarGridSpec(
            num_scalar_prefetch=1,
            grid=(rows // tile,),
            in_specs=[block] * 5 + [pl.BlockSpec((1, depth), lambda i, at: (0, 0))],
            out_specs=block,
        ),
        out_shape=jax.ShapeDtypeStruct((rows, depth), bf16),
        compiler_params=params(),
        cost_estimate=cost(20 * rows * depth, 14 * rows * depth),
        name="first_norm_back",
    )(at, ring, own, swapped, x, d_middle, gain)


def after(value, *others):
    return lax.optimization_barrier((value,) + others)[0]


def shards(
    tokens, gain_attn, w_query, w_key, w_value, w_out, gain_mlp, w_gate, w_up, w_down, cotangent
):
    groups = lax.axis_size("seq")
    dp_count = lax.axis_size("dp")
    seq_count, piece, depth = tokens.shape
    assert seq_count == 1 and groups >= KV and groups % 2 == 0 and groups % dp_count == 0
    assert dp_count & (dp_count - 1) == 0
    length = piece * groups
    width = H // groups * HD
    repeat = groups // KV
    own_rows = w_query.shape[0]
    half = depth // 2
    block = depth // dp_count

    chips = groups // 2
    middle_chip = chips // 2
    order = list(range(middle_chip)) + list(range(chips - 1, middle_chip - 1, -1))
    place = np.argsort(order)
    follow = [order[(place[c] + 1) % chips] for c in range(chips)]
    ring = [(2 * c + k, 2 * follow[c] + k) for c in range(chips) for k in range(2)]
    swap = [(i, i ^ 1) for i in range(groups)]

    seq_at = lax.axis_index("seq")
    dp_at = lax.axis_index("dp")
    core_at = seq_at % 2
    ring_at = jnp.asarray(place, jnp.int32)[seq_at // 2]
    chunk = jnp.asarray(order, jnp.int32)[(ring_at + chips - jnp.arange(chips)) % chips]
    pair_at = 2 * chunk[:, None] + jnp.stack([core_at, 1 - core_at])[None, :]
    dp_order = dp_at ^ jnp.arange(dp_count)
    group_order = (dp_order[:, None] * (groups // dp_count) + jnp.arange(groups // dp_count)).reshape(-1)
    at = jnp.concatenate([core_at[None], jnp.arange(dp_count), group_order]).astype(jnp.int32)

    def step_ring(x):
        return lax.ppermute(x, "seq", ring)

    def step_swap(x):
        return lax.ppermute(x, "seq", swap)

    def step_dp(x, k):
        return lax.ppermute(x, "dp", [(i, i ^ k) for i in range(dp_count)])

    def rows_at(x, start, count):
        return lax.dynamic_slice_in_dim(x, start, count, 0)

    def cols_at(x, start, count):
        return lax.dynamic_slice_in_dim(x, start, count, 1)

    def gather_dp(x):
        return [x] + [step_dp(x, k) for k in range(1, dp_count)]

    def gather_hops(x):
        if dp_count != 4:
            return gather_dp(x)
        cut = x.shape[0] // 2
        one, two = step_dp(x, 1), step_dp(x, 2)
        return [x, one, two, step_dp(one[:cut], 2), step_dp(two[cut:], 1)]

    def scatter_dp(parts):
        return [step_dp(parts[k], k) for k in range(1, dp_count)]

    def full_weight(w):
        return [lax.all_gather(w, "dp", axis=0, tiled=True)]

    def owned_grad(grad):
        return lax.psum_scatter(grad, "dp", scatter_dimension=0, tiled=True)

    def pair_sides(own, got):
        return jnp.where(core_at == 0, jnp.concatenate([own, got]), jnp.concatenate([got, own]))

    x_own = tokens.reshape(piece, depth)
    cot_own = cotangent.reshape(piece, depth)

    def per_group(w):
        return jnp.repeat(w.reshape(own_rows, KV, HD), repeat, axis=1)

    with jax.named_scope("projection_columns"):
        gains_own = jnp.stack([gain_attn, gain_mlp], axis=-1)
        gains_own = jnp.pad(gains_own, ((0, 0), (0, LANES - 2)))
        gains_own = jnp.broadcast_to(gains_own[:, None, :], (own_rows, groups, LANES))
        own_cols = jnp.concatenate(
            [w_query.reshape(own_rows, groups, width), per_group(w_key), per_group(w_value), gains_own],
            axis=-1,
        )
        cols = own_cols.shape[-1]
        dp_rows = groups * own_rows
        cols_dp = lax.all_to_all(jnp.transpose(own_cols, (1, 0, 2)), "seq", 0, 0, tiled=True)
        cols_dp = cols_dp.reshape(dp_rows, cols)

    with jax.named_scope("tokens_ring"):
        x_mine = [x_own, step_ring(after(x_own, own_cols))]

    with jax.named_scope("projection_columns"):
        cols_all = jnp.zeros((depth, cols), bf16)
        for k, part in enumerate(gather_dp(cols_dp)):
            cols_all = lax.dynamic_update_slice_in_dim(cols_all, part, dp_order[k] * dp_rows, 0)
        w_qkv = cols_all[:, : width + 2 * HD]
        gains = jnp.transpose(cols_all[:, width + 2 * HD : width + 2 * HD + 2].astype(f32))
        gain_one, gain_two = gains[:1], gains[1:]

    with jax.named_scope("tokens_ring"):
        for s in range(2, chips):
            x_mine.append(step_ring(after(x_mine[-1], cols_dp if s == 2 else cols_all)))
        x_other = [step_swap(x) for x in x_mine]

    with jax.named_scope("out_weight"):
        keep = cols_at(w_out, core_at * half, half)
        give = cols_at(w_out, (1 - core_at) * half, half)
        chip_rows = [pair_sides(keep, step_swap(give))]

    cos, sin = rope_tables(length)
    held = ()

    def project(s, ahead):
        other = after(x_other[s], ahead)
        return qkv_call(
            pair_at[s], x_mine[s], other, gain_one, cols_all, cos, sin, width, length, held
        )

    for s in range(min(2, chips)):
        held = project(s, chip_rows[0])

    with jax.named_scope("out_weight"):
        chip_rows.append(step_ring(after(chip_rows[0], x_mine[-1], held[0])))
        for _ in range(2, chips):
            chip_rows.append(step_ring(chip_rows[-1]))
        out_rows = jnp.zeros((dp_rows, half), bf16)
        for s in range(chips):
            out_rows = lax.dynamic_update_slice_in_dim(out_rows, chip_rows[s], chunk[s] * 2 * own_rows, 0)

        out_mine = gather_hops(out_rows)
        out_other = [step_swap(p) for p in out_mine]

    with jax.named_scope("feed_forward_weights"):
        gate_full, up_full, down_full = full_weight(w_gate), full_weight(w_up), full_weight(w_down)

    for s in range(2, chips):
        held = project(s, chip_rows[s - 1])
    normed, queries, keys_values = held
    queries = after(queries, chip_rows[-1])

    with jax.named_scope("cotangent_ring"):
        c_mine = [cot_own, step_ring(after(cot_own, chip_rows[-1]))]
        c_other = [step_swap(c) for c in c_mine]

    head_out, out_t, lse = attn_fwd(queries, keys_values)
    with jax.named_scope("mixed"):
        head_out = after(head_out, c_mine[1]).reshape(groups, piece, width)
        mixed = lax.all_to_all(head_out, "seq", 0, 0, tiled=True)
    middle, normed_two = out_call(at, out_mine, out_other, mixed, x_own, gain_two, dp_count)

    def add(*parts):
        total = parts[0].astype(f32)
        for p in parts[1:]:
            total = total + p.astype(f32)
        return total

    def weight_grad(rows, grads):
        return mm(rows, grads, TN).astype(bf16)

    n_mine = [normed_two]
    for s in range(1, chips):
        if s + 1 < chips:
            with jax.named_scope("cotangent_ring"):
                c_mine.append(step_ring(after(c_mine[-1], mixed if s == 1 else n_mine[-1])))
                c_other.append(step_swap(c_mine[-1]))
        with jax.named_scope("normed_ring"):
            n_mine.append(step_ring(n_mine[-1] if s == 1 else after(n_mine[-1], c_mine[-1])))
    with jax.named_scope("normed_ring"):
        n_other = [step_swap(n) for n in n_mine]

    ffn, held, acc = [], (), None
    for s in range(chips):
        n_here = n_other[s] if acc is None else after(n_other[s], acc)
        out = ffn_call(
            s, chips, n_mine[s], n_here, c_mine[s], c_other[s], gate_full, up_full, down_full, held
        )
        held, rest = out[:5], out[5:]
        with jax.named_scope("feed_forward_pair"):
            back_swapped = step_swap(rest[2])
            down_swapped = step_swap(rest[3])
        ffn.append((rest[0], rest[1], back_swapped, down_swapped))
        if s:
            with jax.named_scope("back_ring"):
                so_far = add(ffn[s][0]) if acc is None else add(step_ring(acc), ffn[s][0])
                acc = add(lax.optimization_barrier(so_far), ffn[s][2]).astype(bf16)
    n_all, c_all, hidden, d_gate, d_up = held
    n_all = after(n_all, acc)
    with jax.named_scope("back_ring"):
        back_got = step_ring(acc)

    with jax.named_scope("gate_grad"):
        gate_part = weight_grad(n_all, d_gate)
        grad_gate = owned_grad(gate_part)
    with jax.named_scope("up_grad"):
        up_part = weight_grad(n_all, d_up)
        grad_up = owned_grad(up_part)
    back_got = after(back_got, gate_part, up_part)

    d_middle, branch, d_gain_two, d_mixed = mid_call(
        at, out_mine, out_other, back_got, ffn[0][0], ffn[0][2], middle, cot_own, gain_two, width, dp_count
    )
    with jax.named_scope("d_mixed"):
        d_heads = lax.all_to_all(d_mixed, "seq", 0, 0, tiled=True).reshape(length, width)

    with jax.named_scope("out_grad"):

        def out_part(start):
            g = jnp.einsum("gnh,nd->ghd", mixed, cols_at(branch, start, half), preferred_element_type=f32)
            return g.reshape(groups * width, half).astype(bf16)

        out_theirs = out_part((1 - core_at) * half)
        out_theirs_sent = step_swap(out_theirs)
        out_own = out_part(core_at * half)
    with jax.named_scope("down_grad"):
        down_rows, _ = lax.optimization_barrier((c_all, branch))
        down_part = weight_grad(down_rows, hidden)
        grad_down = owned_grad(down_part)

    with jax.named_scope("down_ring"):
        acc = add(after(ffn[1][1], back_got), ffn[1][3]).astype(bf16)
        down_two = step_ring(acc)

    with jax.named_scope("out_grad"):
        out_sum = add(out_own, out_theirs_sent).astype(bf16)
        out_dp = owned_grad(out_sum)

    d_heads = after(d_heads, down_part, out_sum)

    d_queries, d_kv = attn_bwd(queries, keys_values, d_heads, out_t, lse, cos, sin)

    with jax.named_scope("down_ring"):
        for s in range(2, chips):
            acc = add(after(down_two, d_heads if s == 2 else d_kv), ffn[s][1], ffn[s][3]).astype(bf16)
            down_two = step_ring(acc)

    with jax.named_scope("first_ring"):
        def d_normed(s, side):
            d_q = rows_at(d_queries, pair_at[s, side] * piece, piece)
            d_k = rows_at(d_kv, pair_at[s, side] * piece, piece)
            return mm(jnp.concatenate([d_q, d_k], axis=1), w_qkv, NT).astype(bf16)

        steps = list(range(1, chips)) + [0]
        theirs = {s: step_swap(d_normed(s, 1)) for s in steps}
        own = {s: d_normed(s, 0) for s in steps}
        first_acc = [add(own[1], theirs[1]).astype(bf16)]
        for s in range(2, chips):
            first_acc.append(add(step_ring(first_acc[-1]), own[s], theirs[s]).astype(bf16))
        first_got = step_ring(first_acc[-1])

    with jax.named_scope("projection_grads"):
        d_qkv = jnp.concatenate([d_queries, d_kv], axis=1)
        grad_cols = mm(after(normed, first_acc[0]), d_qkv, TN).astype(bf16)
        high = d_gain_two.astype(bf16)
        rest = (d_gain_two - high.astype(f32)).astype(bf16)
        extra = jnp.pad(jnp.transpose(jnp.concatenate([high, rest], axis=0)), ((0, 0), (0, LANES - 2)))
        grad_cols = jnp.concatenate([grad_cols, extra], axis=1)
        col_parts = [rows_at(grad_cols, dp_order[k] * block, block) for k in range(dp_count)]
        col_sent = [after(p, first_acc[1]) for p in scatter_dp(col_parts)]
        total = add(col_parts[0], *col_sent).astype(bf16)
        dealt = lax.all_to_all(total.reshape(groups, own_rows, cols), "seq", 0, 0, tiled=True)

    with jax.named_scope("feed_forward_grads"):
        grads = lax.optimization_barrier((grad_gate, grad_up, grad_down, first_acc[-1]))
        grad_gate, grad_up, grad_down = (g.astype(f32) for g in grads[:3])

    with jax.named_scope("out_grad"):
        same_core = [[2 * c + k for c in range(chips)] for k in range(2)]
        out_dp = after(out_dp, first_acc[-1]).reshape(chips, 2 * own_rows, half)
        out_terms = lax.all_to_all(out_dp, "seq", 0, 0, axis_index_groups=same_core, tiled=True)
        acc = jnp.sum(out_terms.astype(f32), axis=0)
        out_keep = rows_at(acc, core_at * own_rows, own_rows)
        out_give = rows_at(acc, (1 - core_at) * own_rows, own_rows).astype(bf16)
        out_take = step_swap(out_give).astype(f32)
        grad_out = jnp.where(
            core_at == 0,
            jnp.concatenate([out_keep, out_take], axis=1),
            jnp.concatenate([out_take, out_keep], axis=1),
        )

    grad_tokens = first_call(at, first_got, own[0], theirs[0], x_own, d_middle, gain_one, dp_count)
    block_out = (middle + add(down_two, ffn[0][1], ffn[0][3])).astype(bf16)

    def join(x):
        return jnp.transpose(x, (1, 0, 2)).reshape(own_rows, -1)

    def fold(x):
        return join(jnp.sum(x.reshape(KV, repeat, own_rows, HD), axis=1))

    dealt = after(dealt, first_acc[-1]).astype(f32)
    grad_query = join(dealt[:, :, :width])
    grad_key = fold(dealt[:, :, width : width + HD])
    grad_value = fold(dealt[:, :, width + HD : width + 2 * HD])
    grad_gain_two = jnp.sum(dealt[:, :, width + 2 * HD : width + 2 * HD + 2], axis=(0, 2))

    def against(w, grad):
        return jnp.sum(w.astype(f32) * grad, axis=1)

    grad_gain_one = against(w_query, grad_query) + against(w_key, grad_key) + against(w_value, grad_value)
    grad_gain_one = grad_gain_one / gain_attn.astype(f32)

    return (
        block_out.reshape(1, piece, depth),
        grad_tokens.reshape(1, piece, depth),
        grad_gain_one,
        grad_query,
        grad_key,
        grad_value,
        grad_out,
        grad_gain_two,
        grad_gate,
        grad_up,
        grad_down,
    )


def solution(mesh):
    rows = P("dp", "seq", None)
    both = P(("dp", "seq"))
    flat = P(("dp", "seq"), None)
    tiles = P("dp", "seq")
    in_specs = (rows, both, flat, flat, flat, flat, both, tiles, tiles, tiles, rows)
    out_specs = (rows, rows, both, flat, flat, flat, flat, both, tiles, tiles, tiles)
    return jax.shard_map(shards, mesh=mesh, in_specs=in_specs, out_specs=out_specs, check_vma=False)
```
